32 devices in a mesh: cuts: 2 (over y), wide: 8 (over z, x), narrow: 2 (over core).
Axes of the slice: x: 2, y: 2, z: 4, core: 2. Of those that a mesh axis runs over, the one named last changes fastest.
Arguments:
- stem_tensor: float32 [2, 4194304], P(None, ('cuts', 'wide', 'narrow')), parts along dimension 1, may hold values from -6 to 6
- sub_branches: bfloat16 [3, 2, 2, 512, 512], P(None, 'narrow', None, 'wide'), may hold values from -0.1875 to 0.1875
- branch_bits: int32 [3, 9], replicated, may hold values from 7 to 20, as said below
Outputs:
- amplitudes: float32 [2, 4194304], P(None, ('cuts', 'wide', 'narrow')), parts along dimension 1
The draws below stay inside these ranges and needn't reach their ends.
There are 2 independent parts, one for each index of `cuts`. The reference program is written for one: setup_inputs(seed, part) draws one part's arguments, and reference() takes and returns one part's arrays. A program takes and returns all parts, laid end to end along the dimension named above; an argument that names none is the same for every part. Nothing has to cross between parts.
Inputs may be any that keep to these rules, and one draw needn't show every extreme that they name: `branch_bits`: no bit below 7 is ever named. Row 0 holds 9 distinct bits of 7 to 16, bit 7 among them. Row 1 holds the 3 bits 17 + 1 to 20 and 6 distinct bits of 7 to 12. Row 2 holds bit 17 and 8 distinct bits of 7 to 12 and 18 to 20. Each row in any order.
All inputs are finite; a program needn't handle non-finite values.
Results may differ from the reference program's by a relative error of at most 0.005.
Values may be sent and summed in bfloat16 or wider, within the bound.
A program may use at most 64 MiB of HBM per device.

```python
import jax
import jax.numpy as jnp
from jax import lax

LBITS = 17
BBITS = 9
BRANCHES = 3
BDIM = 512
WBITS = 3
QBITS = 21
STEM = 2097152


def draw_branch_bits(key, part):
    subkeys = jax.random.split(key, 6)
    wide_positions = jnp.arange(LBITS + 1, LBITS + WBITS + 1, dtype=jnp.int32)
    first_pick = jax.random.permutation(subkeys[0], LBITS - 8)[:BBITS - 1].astype(jnp.int32) + 8
    first_set = jax.random.permutation(subkeys[1], jnp.concatenate([jnp.full((1,), 7, jnp.int32), first_pick]))
    low_pick = jax.random.permutation(subkeys[2], LBITS - WBITS - 8)[:BBITS - WBITS].astype(jnp.int32) + 7
    second_set = jax.random.permutation(subkeys[3], jnp.concatenate([wide_positions, low_pick]))
    third_pool = jnp.concatenate([jnp.arange(7, LBITS - WBITS - 1, dtype=jnp.int32), wide_positions])
    third_pick = third_pool[jax.random.permutation(subkeys[4], third_pool.shape[0])[:BBITS - 1]]
    third_set = jax.random.permutation(subkeys[5], jnp.concatenate([jnp.full((1,), LBITS, jnp.int32), third_pick]))
    return jnp.stack([first_set, second_set, third_set]).astype(jnp.int32)


def level_of(own_key, dims, shards, low, largest):
    def one(axis_at, blocks):
        heights = jax.random.uniform(jax.random.fold_in(jax.random.fold_in(own_key, 6), axis_at), (blocks,), jnp.float32, low / len(shards), largest / len(shards))
        return jnp.repeat(jnp.exp(heights), dims[axis_at] // blocks).reshape((-1,) + (1,) * (len(dims) - axis_at - 1))

    loudness = one(*shards[0])
    for cut in shards[1:]:
        loudness = loudness * one(*cut)
    return loudness


def gaussian(key, dims, width, limit, shards=(), kind=jnp.bfloat16):
    result = jax.random.normal(key, dims, jnp.float32) * width
    if len(shards) > 0:
        result = level_of(key, dims, shards, -0.22, 0.18) * result
    return jnp.clip(result, min=-limit, max=limit).astype(kind)


def setup_inputs(seed: int = 0, part: int = 0) -> dict:
    arg_keys = jax.random.split(jax.random.key(seed), 4)
    part_splits = jax.random.split(jax.random.fold_in(arg_keys[3], part), 4)
    return {
        "stem_tensor": gaussian(part_splits[0], (2, STEM), 1.0, 6.0, ((1, 16),), jnp.float32),
        "sub_branches": gaussian(arg_keys[1], (BRANCHES, 2, 2, BDIM, BDIM), (2 * BDIM) ** -0.5, 0.1875, ((1, 2), (3, 8))),
        "branch_bits": draw_branch_bits(jax.random.fold_in(arg_keys[3], 71), part),
    }


def bit_tables(chosen_bits, total_bits, width_bits):
    chosen_bits = chosen_bits.astype(jnp.int32)
    places = jnp.arange(total_bits, dtype=jnp.int32)
    orders = jnp.arange(width_bits, dtype=jnp.int32)
    matches = places[:, None] == chosen_bits[None, :]
    chosen = jnp.any(matches, axis=1)
    ranking = jnp.sum(jnp.where(matches, orders[None, :], 0), axis=1).astype(jnp.int32)
    unchosen = 1 - chosen.astype(jnp.int32)
    free_rank = (jnp.cumsum(unchosen) - unchosen).astype(jnp.int32)
    unit_ones = jnp.ones((total_bits,), jnp.int32)
    weight = jnp.where(chosen, jnp.left_shift(unit_ones, width_bits - 1 - ranking), jnp.left_shift(unit_ones, width_bits + free_rank))
    low_bits = total_bits // 2

    def partial_table(count, first_place, last_place):
        values = jnp.arange(count, dtype=jnp.int32)
        running = jnp.zeros((count,), jnp.int32)
        for position in range(first_place, last_place):
            running = running + jnp.bitwise_and(jnp.right_shift(values, position - first_place), 1) * weight[position]
        return running

    inverse = (partial_table(2 ** (total_bits - low_bits), low_bits, total_bits)[:, None] + partial_table(2 ** low_bits, 0, low_bits)[None, :]).reshape(-1)
    columns = jnp.arange(2 ** width_bits, dtype=jnp.int32)
    col_part = jnp.zeros((2 ** width_bits,), jnp.int32)
    for slot_no in range(width_bits):
        col_part = col_part + jnp.left_shift(jnp.bitwise_and(jnp.right_shift(columns, width_bits - 1 - slot_no), 1), chosen_bits[slot_no])
    row_ids = jnp.arange(2 ** (total_bits - width_bits), dtype=jnp.int32)
    row_part = jnp.zeros((2 ** (total_bits - width_bits),), jnp.int32)
    for position in range(total_bits):
        bit_value = jnp.bitwise_and(jnp.right_shift(row_ids, free_rank[position]), 1) * (2 ** position)
        row_part = row_part + jnp.where(chosen[position], 0, bit_value)
    gather_index = row_part[:, None] + col_part[None, :]
    return gather_index, inverse


def merge_branch(left_factor, right_factor):
    def half_product(first_matrix, second_matrix):
        return jnp.dot(first_matrix, second_matrix, preferred_element_type=jnp.float32)

    real_part = half_product(left_factor[0], right_factor[0]) - half_product(left_factor[1], right_factor[1])
    imag_part = half_product(left_factor[0], right_factor[1]) + half_product(left_factor[1], right_factor[0])
    return jnp.stack([real_part, imag_part]).astype(jnp.bfloat16)


def contract(amplitude, branch, gather_index, inverse):
    picked = jnp.take(amplitude, gather_index, axis=1)
    widened = branch.astype(jnp.float32)

    def real_product(data, matrix):
        return lax.dot_general(data, matrix, (((1,), (1,)), ((), ())), precision=lax.Precision.HIGHEST, preferred_element_type=jnp.float32)

    real_part = real_product(picked[0], widened[0]) - real_product(picked[1], widened[1])
    imag_part = real_product(picked[0], widened[1]) + real_product(picked[1], widened[0])
    merged = jnp.stack([real_part, imag_part]).reshape(2, -1)
    return jnp.take(merged, inverse, axis=1)


def reference(stem_tensor, sub_branches, branch_bits):
    amplitude = stem_tensor
    for which in range(BRANCHES):
        branch = merge_branch(sub_branches[which, 0], sub_branches[which, 1])
        gather_index, inverse = bit_tables(branch_bits[which], QBITS, BBITS)
        amplitude = contract(amplitude, branch, gather_index, inverse)
    return amplitude
```

```python
import functools

import jax
import jax.numpy as jnp
from jax import lax
from jax.experimental import pallas as pl
from jax.experimental.pallas import tpu as pltpu
from jax.sharding import PartitionSpec as P

LBITS = 17
BBITS = 9
BRANCHES = 3


lane_bits = 7


def partner(value, axis, stride):
    mask = 2**stride
    pairs = [(source, source ^ mask) for source in range(lax.axis_size(axis))]
    return lax.ppermute(value, axis, pairs)


def bit_tables(chosen_bits, total_bits, width_bits):
    places = jnp.arange(total_bits, dtype=jnp.int32)
    orders = jnp.arange(width_bits, dtype=jnp.int32)
    matches = places[:, None] == chosen_bits[None, :]
    chosen = jnp.any(matches, axis=1)
    ranking = jnp.sum(jnp.where(matches, orders[None, :], 0), axis=1)
    unchosen = 1 - chosen.astype(jnp.int32)
    free_rank = jnp.cumsum(unchosen) - unchosen
    unit_ones = jnp.ones((total_bits,), jnp.int32)
    weight = jnp.where(
        chosen,
        jnp.left_shift(unit_ones, width_bits - 1 - ranking),
        jnp.left_shift(unit_ones, width_bits + free_rank),
    )
    low_bits = total_bits // 2

    def partial_table(count, first_place, last_place):
        values = jnp.arange(count, dtype=jnp.int32)
        running = jnp.zeros((count,), jnp.int32)
        for position in range(first_place, last_place):
            running = (
                running
                + jnp.bitwise_and(jnp.right_shift(values, position - first_place), 1)
                * weight[position]
            )
        return running

    inverse = (
        partial_table(2 ** (total_bits - low_bits), low_bits, total_bits)[:, None]
        + partial_table(2**low_bits, 0, low_bits)[None, :]
    ).reshape(-1)
    columns = jnp.arange(2**width_bits, dtype=jnp.int32)
    col_part = jnp.zeros((2**width_bits,), jnp.int32)
    for slot_no in range(width_bits):
        col_part = col_part + jnp.left_shift(
            jnp.bitwise_and(jnp.right_shift(columns, width_bits - 1 - slot_no), 1),
            chosen_bits[slot_no],
        )
    row_ids = jnp.arange(2 ** (total_bits - width_bits), dtype=jnp.int32)
    row_part = jnp.zeros((2 ** (total_bits - width_bits),), jnp.int32)
    for position in range(total_bits):
        bit_value = jnp.bitwise_and(jnp.right_shift(row_ids, free_rank[position]), 1) * 2**position
        row_part = row_part + jnp.where(chosen[position], 0, bit_value)
    gather_index = row_part[:, None] + col_part[None, :]
    return (gather_index, inverse)


def half_product(first_matrix, second_matrix):
    return jnp.dot(first_matrix, second_matrix, preferred_element_type=jnp.float32)


def merge_branch(left_factor, right_factor):
    real_part = half_product(left_factor[0], right_factor[0]) - half_product(
        left_factor[1], right_factor[1]
    )
    imag_part = half_product(left_factor[0], right_factor[1]) + half_product(
        left_factor[1], right_factor[0]
    )
    return jnp.stack([real_part, imag_part]).astype(jnp.bfloat16)


def contract_blocks(amplitude, branch, gather_index, inverse):
    lanes = 2**lane_bits
    blocks = amplitude.reshape(2, -1, lanes)
    picked = jnp.take(blocks, gather_index, axis=1)
    widened = branch.astype(jnp.float32)

    def real_product(data, matrix):
        return jnp.einsum(
            "rul,cu->rcl",
            data,
            matrix,
            precision=lax.Precision.HIGHEST,
            preferred_element_type=jnp.float32,
        )

    real_part = real_product(picked[0], widened[0]) - real_product(picked[1], widened[1])
    imag_part = real_product(picked[0], widened[1]) + real_product(picked[1], widened[0])
    merged = jnp.stack([real_part, imag_part]).reshape(2, -1, lanes)
    return jnp.take(merged, inverse, axis=1).reshape(2, -1)


def shards(stem_tensor, sub_branches, branch_bits):
    wide_count = lax.axis_size("wide")
    wide_log = wide_count.bit_length() - 1
    local_bits = LBITS
    block_shape = (2, wide_count, 2, stem_tensor.shape[1] // (2 * wide_count))
    leading = lax.axis_index("narrow") == 0

    def move_wide(amplitude):
        return lax.all_to_all(
            amplitude.reshape(block_shape), "wide", split_axis=1, concat_axis=1, tiled=True
        ).reshape(2, -1)

    def move_narrow(amplitude):
        return lax.all_to_all(
            amplitude.reshape(block_shape), "narrow", split_axis=2, concat_axis=2, tiled=True
        ).reshape(2, -1)

    def working_places(which):
        chosen_bits = branch_bits[which]
        if which == 0:
            return chosen_bits - lane_bits
        shifted = jnp.where(chosen_bits == local_bits, local_bits - wide_log - 1, chosen_bits)
        placed = jnp.where(chosen_bits > local_bits, chosen_bits - wide_log - 1, shifted)
        return placed - lane_bits

    amplitude = stem_tensor
    for which in range(BRANCHES):
        own_rows = sub_branches[which, 0]
        own_whole = lax.all_gather(own_rows, "wide", axis=1, tiled=True)
        partner_whole = partner(own_whole, "narrow", 0)
        branch = merge_branch(
            jnp.where(leading, own_whole, partner_whole),
            jnp.where(leading, partner_whole, own_whole),
        )
        if which == 1:
            amplitude = move_wide(amplitude)
        if which == 2:
            amplitude = move_narrow(amplitude)
        gather_index, inverse = bit_tables(working_places(which), local_bits - lane_bits, BBITS)
        amplitude = contract_blocks(amplitude, branch, gather_index, inverse)
    amplitude = move_narrow(amplitude)
    amplitude = move_wide(amplitude)
    return amplitude


MESH = pl.DeviceIdType.MESH


def ring_place(wide, count):
    return wide // 2 + (wide % 2) * (count - 1 - 2 * (wide // 2))


def ring_member(place, count):
    back = place // (count // 2)
    return 2 * place + back * (2 * (count - 1 - place) + 1 - 2 * place)


def stem_kernel(
    count, places_ref, stem_ref, sub_ref, out_ref,
    gath, bcat, work, prod, send, recv,
    own_sem, ring_send, ring_recv, pair_send, pair_recv, swap_send, swap_recv,
):
    wide = lax.axis_index("wide")
    narrow = lax.axis_index("narrow")
    rows = sub_ref.shape[2]
    branches = sub_ref.shape[0]
    dim = bcat.shape[0]
    total = stem_ref.shape[0]
    bits = total.bit_length() - 1
    half = count // 2
    lanes = stem_ref.shape[1] // 2
    place = ring_place(wide, count)
    neighbours = (
        ring_member((place + 1) % count, count),
        ring_member((place + count - 1) % count, count),
    )
    members = 2 * count
    me = wide * 2 + narrow
    piece = total // members

    barrier = pltpu.get_barrier_semaphore()
    for neighbour in neighbours:
        pl.semaphore_signal(barrier, inc=1, device_id={"wide": neighbour}, device_id_type=MESH)
    pl.semaphore_signal(barrier, inc=1, device_id={"narrow": 1 - narrow}, device_id_type=MESH)
    pl.semaphore_wait(barrier, 3)

    def block_rows(offset):
        origin = ring_member((place + count - offset) % count, count)
        return pl.ds(pl.multiple_of(origin * rows, rows), rows)

    def used(way, part, distance):
        return distance < half or (distance == half and part == way)

    def offset_of(way, distance):
        return distance if way == 0 else (count - distance) % count

    started = []

    def ring_copy(way, which, part, distance):
        target = gath.at[narrow, which, part, block_rows(offset_of(way, distance - 1))]
        return pltpu.make_async_remote_copy(
            src_ref=sub_ref.at[which, part] if distance == 1 else target,
            dst_ref=target,
            send_sem=ring_send.at[way, which, part, distance - 1],
            recv_sem=ring_recv.at[way, which, part, distance - 1],
            device_id={"wide": neighbours[way]},
            device_id_type=MESH,
        )

    def pair_copy(which, part, offset):
        target = gath.at[narrow, which, part, block_rows(offset)]
        return pltpu.make_async_remote_copy(
            src_ref=sub_ref.at[which, part] if offset == 0 else target,
            dst_ref=target,
            send_sem=pair_send.at[which, part, offset],
            recv_sem=pair_recv.at[which, part, offset],
            device_id={"narrow": 1 - narrow},
            device_id_type=MESH,
        )

    def launch(copy):
        copy.start()
        started.append(copy)

    own_copies = []

    def send_own(which):
        for part in range(2):
            for way in range(2):
                if used(way, part, 1):
                    launch(ring_copy(way, which, part, 1))
        for part in range(2):
            launch(pair_copy(which, part, 0))
            keep = pltpu.make_async_copy(
                sub_ref.at[which, part],
                gath.at[narrow, which, part, block_rows(0)],
                own_sem.at[which, part],
            )
            keep.start()
            own_copies.append(keep)

    def relay(which):
        for distance in range(1, half + 1):
            for part in range(2):
                for way in range(2):
                    if not used(way, part, distance):
                        continue
                    ring_copy(way, which, part, distance).wait_recv()
                    if used(way, part, distance + 1):
                        launch(ring_copy(way, which, part, distance + 1))
                    launch(pair_copy(which, part, offset_of(way, distance)))
            if distance == max(half - 1, 1) and which + 1 < branches:
                send_own(which + 1)
        for part in range(2):
            own_copies[2 * which + part].wait()
            for offset in range(count):
                pair_copy(which, part, offset).wait_recv()

    def merge(which):
        first = [gath[0, which, part] for part in range(2)]
        second = [gath[1, which, part] for part in range(2)]

        def half_product(left, right):
            return jnp.dot(left, right, preferred_element_type=jnp.float32)

        bcat[:, :dim] = (
            half_product(first[0], second[0]) - half_product(first[1], second[1])
        ).astype(jnp.bfloat16)
        bcat[:, dim:] = (
            half_product(first[0], second[1]) + half_product(first[1], second[0])
        ).astype(jnp.bfloat16)

    width = dim.bit_length() - 1

    def free_place(which):
        rest = bits * (bits - 1) // 2
        for slot in range(width):
            rest = rest - places_ref[which, slot]
        return rest

    def bit_at(values, position):
        return jnp.bitwise_and(jnp.right_shift(values, position), 1)

    def gathered_place(which, values):
        found = jnp.left_shift(bit_at(values, free_place(which)), width)
        for slot in range(width):
            found = found + jnp.left_shift(
                bit_at(values, places_ref[which, slot]), width - 1 - slot
            )
        return found

    def natural_place(which, values):
        found = jnp.left_shift(bit_at(values, width), free_place(which))
        for slot in range(width):
            found = found + jnp.left_shift(
                bit_at(values, width - 1 - slot), places_ref[which, slot]
            )
        return found

    def permute(source, target_ref, goal):
        step = min(256, total)
        for first in range(0, total, step):
            index = lax.broadcasted_iota(jnp.int32, (step, total), 0) + first
            onehot = (index == goal).astype(jnp.float32).astype(jnp.bfloat16)
            target_ref[first:first + step, :] = jnp.dot(
                onehot, source, preferred_element_type=jnp.float32
            ).astype(jnp.bfloat16)

    def contract():
        for first in range(0, total, dim):
            data = work[first:first + dim, :]
            turned = jnp.concatenate([-data[:, lanes:], data[:, :lanes]], axis=1)
            both = jnp.concatenate([data, turned], axis=0)
            prod[first:first + dim, :] = jnp.dot(
                bcat[...], both, preferred_element_type=jnp.float32
            ).astype(jnp.bfloat16)

    def swap_copy(round_no, step):
        other = (me + step) % members
        return pltpu.make_async_remote_copy(
            src_ref=send.at[round_no, pl.ds(pl.multiple_of(other * piece, piece), piece)],
            dst_ref=recv.at[round_no, pl.ds(pl.multiple_of(me * piece, piece), piece)],
            send_sem=swap_send.at[round_no, step],
            recv_sem=swap_recv.at[round_no, step],
            device_id={"wide": other // 2, "narrow": other % 2},
            device_id_type=MESH,
        )

    def swap_start(round_no):
        for step in range(1, members):
            launch(swap_copy(round_no, step))
        mine = pl.ds(pl.multiple_of(me * piece, piece), piece)
        recv[round_no, mine, :] = send[round_no, mine, :]

    def swap_wait(round_no):
        for step in range(1, members):
            swap_copy(round_no, step).wait_recv()

    line = lax.broadcasted_iota(jnp.int32, (1, total), 1)
    send_own(0)
    permute(stem_ref[...], work, gathered_place(0, line))
    relay(0)
    merge(0)
    contract()
    permute(prod[...], send.at[0], natural_place(0, line))
    swap_start(0)
    relay(1)
    merge(1)
    swap_wait(0)
    permute(recv[0], work, gathered_place(1, line))
    contract()
    permute(prod[...], work, gathered_place(2, natural_place(1, line)))
    relay(2)
    merge(2)
    contract()
    permute(prod[...], send.at[1], natural_place(2, line))
    swap_start(1)
    swap_wait(1)
    out_ref[0] = recv[1, :, :lanes].astype(jnp.float32)
    out_ref[1] = recv[1, :, lanes:].astype(jnp.float32)
    for copy in started:
        copy.wait_send()


def shards_in_kernel(stem_tensor, sub_branches, branch_bits):
    count = lax.axis_size("wide")
    wide_log = count.bit_length() - 1
    lanes = 2**lane_bits
    total = stem_tensor.shape[1] // lanes
    bits = total.bit_length() - 1
    dim = sub_branches.shape[-1]
    half = count // 2
    places = jnp.where(
        branch_bits < LBITS,
        branch_bits - lane_bits,
        branch_bits - LBITS + bits - 1 - wide_log,
    )
    stem = (
        stem_tensor.astype(jnp.bfloat16)
        .reshape(2, total, lanes)
        .transpose(1, 0, 2)
        .reshape(total, 2 * lanes)
    )
    vmem = pl.BlockSpec(memory_space=pltpu.VMEM)
    result = pl.pallas_call(
        functools.partial(stem_kernel, count),
        out_shape=jax.ShapeDtypeStruct((2, total, lanes), jnp.float32),
        in_specs=[pl.BlockSpec(memory_space=pltpu.SMEM), vmem, vmem],
        out_specs=vmem,
        scratch_shapes=[
            pltpu.VMEM((2, BRANCHES, 2, dim, dim), jnp.bfloat16),
            pltpu.VMEM((dim, 2 * dim), jnp.bfloat16),
            pltpu.VMEM((total, 2 * lanes), jnp.bfloat16),
            pltpu.VMEM((total, 2 * lanes), jnp.bfloat16),
            pltpu.VMEM((2, total, 2 * lanes), jnp.bfloat16),
            pltpu.VMEM((2, total, 2 * lanes), jnp.bfloat16),
            pltpu.SemaphoreType.DMA((BRANCHES, 2)),
            pltpu.SemaphoreType.DMA((2, BRANCHES, 2, half)),
            pltpu.SemaphoreType.DMA((2, BRANCHES, 2, half)),
            pltpu.SemaphoreType.DMA((BRANCHES, 2, count)),
            pltpu.SemaphoreType.DMA((BRANCHES, 2, count)),
            pltpu.SemaphoreType.DMA((2, 2 * count)),
            pltpu.SemaphoreType.DMA((2, 2 * count)),
        ],
        compiler_params=pltpu.CompilerParams(collective_id=0, has_side_effects=True),
    )(places, stem, sub_branches[:, 0])
    return result.reshape(2, -1)


sublane_tile = 16


def solution(mesh):
    in_specs = (P(None, ("cuts", "wide", "narrow")), P(None, "narrow", None, "wide", None), P())
    out_specs = P(None, ("cuts", "wide", "narrow"))

    def run(stem_tensor, sub_branches, branch_bits):
        whole_tiles = sub_branches.shape[3] % sublane_tile == 0
        body = shards_in_kernel if whole_tiles else shards
        return body(stem_tensor, sub_branches, branch_bits)

    return jax.shard_map(run, mesh=mesh, in_specs=in_specs, out_specs=out_specs, check_vma=False)
```

```python
import functools

import jax
import jax.numpy as jnp
from jax import lax
from jax.experimental import pallas as pl
from jax.experimental.pallas import tpu as pltpu
from jax.sharding import PartitionSpec as P

LBITS = 17
BBITS = 9
BRANCHES = 3


lane_bits = 7


def partner(value, axis, stride):
    mask = 2**stride
    pairs = [(source, source ^ mask) for source in range(lax.axis_size(axis))]
    return lax.ppermute(value, axis, pairs)


def bit_tables(chosen_bits, total_bits, width_bits):
    places = jnp.arange(total_bits, dtype=jnp.int32)
    orders = jnp.arange(width_bits, dtype=jnp.int32)
    matches = places[:, None] == chosen_bits[None, :]
    chosen = jnp.any(matches, axis=1)
    ranking = jnp.sum(jnp.where(matches, orders[None, :], 0), axis=1)
    unchosen = 1 - chosen.astype(jnp.int32)
    free_rank = jnp.cumsum(unchosen) - unchosen
    unit_ones = jnp.ones((total_bits,), jnp.int32)
    weight = jnp.where(
        chosen,
        jnp.left_shift(unit_ones, width_bits - 1 - ranking),
        jnp.left_shift(unit_ones, width_bits + free_rank),
    )
    low_bits = total_bits // 2

    def partial_table(count, first_place, last_place):
        values = jnp.arange(count, dtype=jnp.int32)
        running = jnp.zeros((count,), jnp.int32)
        for position in range(first_place, last_place):
            running = (
                running
                + jnp.bitwise_and(jnp.right_shift(values, position - first_place), 1)
                * weight[position]
            )
        return running

    inverse = (
        partial_table(2 ** (total_bits - low_bits), low_bits, total_bits)[:, None]
        + partial_table(2**low_bits, 0, low_bits)[None, :]
    ).reshape(-1)
    columns = jnp.arange(2**width_bits, dtype=jnp.int32)
    col_part = jnp.zeros((2**width_bits,), jnp.int32)
    for slot_no in range(width_bits):
        col_part = col_part + jnp.left_shift(
            jnp.bitwise_and(jnp.right_shift(columns, width_bits - 1 - slot_no), 1),
            chosen_bits[slot_no],
        )
    row_ids = jnp.arange(2 ** (total_bits - width_bits), dtype=jnp.int32)
    row_part = jnp.zeros((2 ** (total_bits - width_bits),), jnp.int32)
    for position in range(total_bits):
        bit_value = jnp.bitwise_and(jnp.right_shift(row_ids, free_rank[position]), 1) * 2**position
        row_part = row_part + jnp.where(chosen[position], 0, bit_value)
    gather_index = row_part[:, None] + col_part[None, :]
    return (gather_index, inverse)


def half_product(first_matrix, second_matrix):
    return jnp.dot(first_matrix, second_matrix, preferred_element_type=jnp.float32)


def merge_branch(left_factor, right_factor):
    real_part = half_product(left_factor[0], right_factor[0]) - half_product(
        left_factor[1], right_factor[1]
    )
    imag_part = half_product(left_factor[0], right_factor[1]) + half_product(
        left_factor[1], right_factor[0]
    )
    return jnp.stack([real_part, imag_part]).astype(jnp.bfloat16)


def contract_blocks(amplitude, branch, gather_index, inverse):
    lanes = 2**lane_bits
    blocks = amplitude.reshape(2, -1, lanes)
    picked = jnp.take(blocks, gather_index, axis=1)
    widened = branch.astype(jnp.float32)

    def real_product(data, matrix):
        return jnp.einsum(
            "rul,cu->rcl",
            data,
            matrix,
            precision=lax.Precision.HIGHEST,
            preferred_element_type=jnp.float32,
        )

    real_part = real_product(picked[0], widened[0]) - real_product(picked[1], widened[1])
    imag_part = real_product(picked[0], widened[1]) + real_product(picked[1], widened[0])
    merged = jnp.stack([real_part, imag_part]).reshape(2, -1, lanes)
    return jnp.take(merged, inverse, axis=1).reshape(2, -1)


def shards(stem_tensor, sub_branches, branch_bits):
    wide_count = lax.axis_size("wide")
    wide_log = wide_count.bit_length() - 1
    local_bits = LBITS
    block_shape = (2, wide_count, 2, stem_tensor.shape[1] // (2 * wide_count))
    leading = lax.axis_index("narrow") == 0

    def move_wide(amplitude):
        return lax.all_to_all(
            amplitude.reshape(block_shape), "wide", split_axis=1, concat_axis=1, tiled=True
        ).reshape(2, -1)

    def move_narrow(amplitude):
        return lax.all_to_all(
            amplitude.reshape(block_shape), "narrow", split_axis=2, concat_axis=2, tiled=True
        ).reshape(2, -1)

    def working_places(which):
        chosen_bits = branch_bits[which]
        if which == 0:
            return chosen_bits - lane_bits
        shifted = jnp.where(chosen_bits == local_bits, local_bits - wide_log - 1, chosen_bits)
        placed = jnp.where(chosen_bits > local_bits, chosen_bits - wide_log - 1, shifted)
        return placed - lane_bits

    amplitude = stem_tensor
    for which in range(BRANCHES):
        own_rows = sub_branches[which, 0]
        own_whole = lax.all_gather(own_rows, "wide", axis=1, tiled=True)
        partner_whole = partner(own_whole, "narrow", 0)
        branch = merge_branch(
            jnp.where(leading, own_whole, partner_whole),
            jnp.where(leading, partner_whole, own_whole),
        )
        if which == 1:
            amplitude = move_wide(amplitude)
        if which == 2:
            amplitude = move_narrow(amplitude)
        gather_index, inverse = bit_tables(working_places(which), local_bits - lane_bits, BBITS)
        amplitude = contract_blocks(amplitude, branch, gather_index, inverse)
    amplitude = move_narrow(amplitude)
    amplitude = move_wide(amplitude)
    return amplitude


MESH = pl.DeviceIdType.MESH


def stem_kernel(
    count, places_ref, stem_ref, sub_ref, out_ref,
    gath, bcat, work, prod, send, recv,
    own_sem, z_send, z_recv, x_send, x_recv, y_send, y_recv,
    pair_send, pair_recv, swap_send, swap_recv,
):
    wide = lax.axis_index("wide")
    narrow = lax.axis_index("narrow")
    cut = lax.axis_index("cuts")
    rows = sub_ref.shape[2]
    branches = sub_ref.shape[0]
    dim = bcat.shape[0]
    total = work.shape[0]
    lanes = work.shape[1] // 2
    bits = total.bit_length() - 1
    depth = count // 2
    z = wide // 2
    x = wide % 2
    members = 2 * count
    me = wide * 2 + narrow
    piece = total // members

    barrier = pltpu.get_barrier_semaphore()
    for target in ({"wide": 2 * z + 1 - x}, {"cuts": 1 - cut}, {"narrow": 1 - narrow}):
        pl.semaphore_signal(barrier, inc=1, device_id=target, device_id_type=MESH)

    @pl.when(z + 1 < depth)
    def _():
        pl.semaphore_signal(barrier, inc=1, device_id={"wide": wide + 2}, device_id_type=MESH)

    @pl.when(z > 0)
    def _():
        pl.semaphore_signal(barrier, inc=1, device_id={"wide": wide - 2}, device_id_type=MESH)

    pl.semaphore_wait(barrier, 3 + jnp.minimum(z, 1) + jnp.minimum(depth - 1 - z, 1))

    started = []
    own_copies = []

    def there(way, distance):
        return z >= distance if way == 0 else z + distance < depth

    def level(way, distance):
        return z - distance if way == 0 else z + distance

    def slot_of(way, distance):
        return 0 if distance == 0 else 1 + way * (depth - 1) + distance - 1

    def part_of(side):
        return cut if side == 0 else 1 - cut

    def copy_of(which, side, column, way, distance, send_sem, recv_sem, device_id):
        origin = 2 * level(way, distance) + (x if column == 0 else 1 - x)
        span = pl.ds(pl.multiple_of(origin * rows, rows), rows)
        target = gath.at[narrow, which, part_of(side), span]
        own = distance == 0 and column == 0
        return pltpu.make_async_remote_copy(
            src_ref=sub_ref.at[which, part_of(side)] if own else target,
            dst_ref=target,
            send_sem=send_sem,
            recv_sem=recv_sem,
            device_id=device_id,
            device_id_type=MESH,
        )

    def z_copy(which, way, distance):
        return copy_of(
            which, 0, 0, way, distance - 1,
            z_send.at[way, which, distance - 1], z_recv.at[way, which, distance - 1],
            {"wide": wide + 2 if way == 0 else wide - 2},
        )

    def x_copy(which, side, way, distance):
        slot = side if distance == 0 else 1 + slot_of(way, distance)
        return copy_of(
            which, side, 0, way, distance,
            x_send.at[which, slot], x_recv.at[which, slot], {"wide": 2 * z + 1 - x},
        )

    def y_copy(which, column, way, distance):
        slot = slot_of(way, distance)
        return copy_of(
            which, 0, column, way, distance,
            y_send.at[which, column, slot], y_recv.at[which, column, slot],
            {"cuts": 1 - cut},
        )

    def pair_copy(which, side, column, way, distance):
        slot = slot_of(way, distance)
        return copy_of(
            which, side, column, way, distance,
            pair_send.at[which, side, column, slot], pair_recv.at[which, side, column, slot],
            {"narrow": 1 - narrow},
        )

    def launch(build, guard=None):
        if guard is None:
            build().start()
        else:
            pl.when(guard)(lambda: build().start())
        started.append((build, guard))

    def finish(build, guard):
        if guard is None:
            build().wait_send()
        else:
            pl.when(guard)(lambda: build().wait_send())

    def await_recv(build, guard=None):
        if guard is None:
            build().wait_recv()
        else:
            pl.when(guard)(lambda: build().wait_recv())

    ways = (0, 1)
    part_sides = (0, 1)
    call = functools.partial

    def send_own(which):
        launch(call(z_copy, which, 0, 1), there(1, 1))
        launch(call(z_copy, which, 1, 1), there(0, 1))
        for side in part_sides:
            launch(call(x_copy, which, side, 0, 0))
        for side in part_sides:
            launch(call(pair_copy, which, side, 0, 0, 0))
            origin = pl.ds(pl.multiple_of(wide * rows, rows), rows)
            keep = pltpu.make_async_copy(
                sub_ref.at[which, side], gath.at[narrow, which, side, origin],
                own_sem.at[which, side],
            )
            keep.start()
            own_copies.append(keep)

    def take_x_own(which):
        for side in part_sides:
            await_recv(call(x_copy, which, side, 0, 0))
            launch(call(pair_copy, which, side, 1, 0, 0))

    def take_z(which, distance):
        for way in ways:
            guard = there(way, distance)
            await_recv(call(z_copy, which, way, distance), guard)
            if distance + 1 < depth:
                launch(
                    call(z_copy, which, way, distance + 1),
                    jnp.logical_and(guard, there(1 - way, 1)),
                )
            launch(call(y_copy, which, 0, way, distance), guard)
            launch(call(x_copy, which, 0, way, distance), guard)
            launch(call(pair_copy, which, 0, 0, way, distance), guard)

    def take_x(which, distance):
        for way in ways:
            guard = there(way, distance)
            await_recv(call(x_copy, which, 0, way, distance), guard)
            launch(call(y_copy, which, 1, way, distance), guard)
            launch(call(pair_copy, which, 0, 1, way, distance), guard)

    def take_y(which, distance):
        for way in ways:
            guard = there(way, distance)
            for column in (0, 1):
                await_recv(call(y_copy, which, column, way, distance), guard)
                launch(call(pair_copy, which, 1, column, way, distance), guard)

    def complete(which):
        for side in part_sides:
            own_copies[2 * which + side].wait()
            for column in (0, 1):
                await_recv(call(pair_copy, which, side, column, 0, 0))
                for way in ways:
                    for distance in range(1, depth):
                        await_recv(
                            call(pair_copy, which, side, column, way, distance),
                            there(way, distance),
                        )

    def relay(which, first, last):
        if first == 1:
            take_x_own(which)
        for distance in range(first, last + 1):
            if distance < depth:
                take_z(which, distance)
                take_x(which, distance)

    def take_mates(which):
        for distance in range(1, depth):
            take_y(which, distance)
        complete(which)

    def merge(which):
        first = [gath[0, which, part] for part in range(2)]
        second = [gath[1, which, part] for part in range(2)]

        def half_product(left, right):
            return jnp.dot(left, right, preferred_element_type=jnp.float32)

        bcat[:, :dim] = (
            half_product(first[0], second[0]) - half_product(first[1], second[1])
        ).astype(jnp.bfloat16)
        bcat[:, dim:] = (
            half_product(first[0], second[1]) + half_product(first[1], second[0])
        ).astype(jnp.bfloat16)

    width = dim.bit_length() - 1

    narrow_place = bits - 1 - (count.bit_length() - 1)

    def named_place(which, slot):
        bit = places_ref[which, slot]
        return bit + jnp.where(bit < LBITS, -lane_bits, narrow_place - LBITS)

    places = [[named_place(which, slot) for slot in range(width)] for which in range(branches)]

    def free_place(which):
        rest = bits * (bits - 1) // 2
        for slot in range(width):
            rest = rest - places[which][slot]
        return rest

    def bit_at(values, position):
        return jnp.bitwise_and(jnp.right_shift(values, position), 1)

    def gathered_place(which, values):
        found = jnp.left_shift(bit_at(values, free_place(which)), width)
        for slot in range(width):
            found = found + jnp.left_shift(
                bit_at(values, places[which][slot]), width - 1 - slot
            )
        return found

    def natural_place(which, values):
        found = jnp.left_shift(bit_at(values, width), free_place(which))
        for slot in range(width):
            found = found + jnp.left_shift(
                bit_at(values, width - 1 - slot), places[which][slot]
            )
        return found

    def permute(source, target_ref, goal):
        step = min(256, total)
        for first in range(0, total, step):
            index = lax.broadcasted_iota(jnp.int32, (step, total), 0) + first
            onehot = (index == goal).astype(jnp.float32).astype(jnp.bfloat16)
            target_ref[first:first + step, :] = jnp.dot(
                onehot, source, preferred_element_type=jnp.float32
            ).astype(jnp.bfloat16)

    def contract():
        for first in range(0, total, dim):
            data = work[first:first + dim, :]
            turned = jnp.concatenate([-data[:, lanes:], data[:, :lanes]], axis=1)
            both = jnp.concatenate([data, turned], axis=0)
            prod[first:first + dim, :] = jnp.dot(
                bcat[...], both, preferred_element_type=jnp.float32
            ).astype(jnp.bfloat16)

    def swap_copy(round_no, step):
        other = (me + step) % members
        return pltpu.make_async_remote_copy(
            src_ref=send.at[round_no, pl.ds(pl.multiple_of(other * piece, piece), piece)],
            dst_ref=recv.at[round_no, pl.ds(pl.multiple_of(me * piece, piece), piece)],
            send_sem=swap_send.at[round_no, step],
            recv_sem=swap_recv.at[round_no, step],
            device_id={"wide": other // 2, "narrow": other % 2},
            device_id_type=MESH,
        )

    far_first = sorted(range(1, members), key=lambda step: -min(step, members - step))

    def swap_start(round_no):
        for step in far_first:
            launch(call(swap_copy, round_no, step))
        mine = pl.ds(pl.multiple_of(me * piece, piece), piece)
        recv[round_no, mine, :] = send[round_no, mine, :]

    def swap_wait(round_no):
        for step in far_first:
            swap_copy(round_no, step).wait_recv()

    line = lax.broadcasted_iota(jnp.int32, (1, total), 1)
    send_own(0)
    stem = jnp.concatenate(
        [stem_ref[pl.ds(part, total, stride=2), :] for part in range(2)], axis=1
    ).astype(jnp.bfloat16)
    permute(stem, work, gathered_place(0, line))
    middle = max(depth - 2, 1)
    relay(0, 1, middle)
    send_own(1)
    relay(0, middle + 1, depth - 1)
    relay(1, 1, 1)
    take_mates(0)
    merge(0)
    contract()
    relay(1, 2, middle)
    permute(prod[...], send.at[0], natural_place(0, line))
    swap_start(0)
    send_own(2)
    relay(1, middle + 1, depth - 1)
    relay(2, 1, 1)
    take_mates(1)
    merge(1)
    relay(2, 2, depth - 1)
    swap_wait(0)
    permute(recv[0], work, gathered_place(1, line))
    contract()
    permute(prod[...], work, gathered_place(2, natural_place(1, line)))
    take_mates(2)
    merge(2)
    contract()
    permute(prod[...], send.at[1], natural_place(2, line))
    swap_start(1)
    swap_wait(1)
    for part in range(2):
        out_ref[pl.ds(part, total, stride=2), :] = recv[
            1, :, part * lanes:(part + 1) * lanes
        ].astype(jnp.float32)
    for build, guard in started:
        finish(build, guard)


def shards_in_kernel(stem_tensor, sub_branches, branch_bits):
    count = lax.axis_size("wide")
    depth = count // 2
    lanes = 2**lane_bits
    total = stem_tensor.shape[1] // lanes
    dim = sub_branches.shape[-1]
    stem = stem_tensor.reshape(2, total, lanes).transpose(1, 0, 2).reshape(2 * total, lanes)
    vmem = pl.BlockSpec(memory_space=pltpu.VMEM)
    slots = 2 * depth - 1
    semaphores = [(BRANCHES, 2)]
    for shape in ((2, BRANCHES, depth), (BRANCHES, slots + 1), (BRANCHES, 2, slots),
                  (BRANCHES, 2, 2, slots), (2, 2 * count)):
        semaphores += [shape, shape]
    result = pl.pallas_call(
        functools.partial(stem_kernel, count),
        out_shape=jax.ShapeDtypeStruct((2 * total, lanes), jnp.float32),
        in_specs=[pl.BlockSpec(memory_space=pltpu.SMEM), vmem, vmem],
        out_specs=vmem,
        scratch_shapes=[
            pltpu.VMEM((2, BRANCHES, 2, dim, dim), jnp.bfloat16),
            pltpu.VMEM((dim, 2 * dim), jnp.bfloat16),
            pltpu.VMEM((total, 2 * lanes), jnp.bfloat16),
            pltpu.VMEM((total, 2 * lanes), jnp.bfloat16),
            pltpu.VMEM((2, total, 2 * lanes), jnp.bfloat16),
            pltpu.VMEM((2, total, 2 * lanes), jnp.bfloat16),
        ] + [pltpu.SemaphoreType.DMA(shape) for shape in semaphores],
        compiler_params=pltpu.CompilerParams(collective_id=0, has_side_effects=True),
    )(branch_bits, stem, sub_branches[:, 0])
    return result.reshape(total, 2, lanes).transpose(1, 0, 2).reshape(2, -1)


sublane_tile = 16


def solution(mesh):
    in_specs = (P(None, ("cuts", "wide", "narrow")), P(None, "narrow", None, "wide", None), P())
    out_specs = P(None, ("cuts", "wide", "narrow"))

    def run(stem_tensor, sub_branches, branch_bits):
        whole_tiles = sub_branches.shape[3] % sublane_tile == 0 and mesh.shape["cuts"] == 2
        body = shards_in_kernel if whole_tiles else shards
        return body(stem_tensor, sub_branches, branch_bits)

    return jax.shard_map(run, mesh=mesh, in_specs=in_specs, out_specs=out_specs, check_vma=False)
```

```python
import functools

import jax
import jax.numpy as jnp
from jax import lax
from jax.experimental import pallas as pl
from jax.experimental.pallas import tpu as pltpu
from jax.sharding import PartitionSpec as P

LBITS = 17
BBITS = 9
BRANCHES = 3


lane_bits = 7


def partner(value, axis, stride):
    mask = 2**stride
    pairs = [(source, source ^ mask) for source in range(lax.axis_size(axis))]
    return lax.ppermute(value, axis, pairs)


def bit_tables(chosen_bits, total_bits, width_bits):
    places = jnp.arange(total_bits, dtype=jnp.int32)
    orders = jnp.arange(width_bits, dtype=jnp.int32)
    matches = places[:, None] == chosen_bits[None, :]
    chosen = jnp.any(matches, axis=1)
    ranking = jnp.sum(jnp.where(matches, orders[None, :], 0), axis=1)
    unchosen = 1 - chosen.astype(jnp.int32)
    free_rank = jnp.cumsum(unchosen) - unchosen
    unit_ones = jnp.ones((total_bits,), jnp.int32)
    weight = jnp.where(
        chosen,
        jnp.left_shift(unit_ones, width_bits - 1 - ranking),
        jnp.left_shift(unit_ones, width_bits + free_rank),
    )
    low_bits = total_bits // 2

    def partial_table(count, first_place, last_place):
        values = jnp.arange(count, dtype=jnp.int32)
        running = jnp.zeros((count,), jnp.int32)
        for position in range(first_place, last_place):
            running = (
                running
                + jnp.bitwise_and(jnp.right_shift(values, position - first_place), 1)
                * weight[position]
            )
        return running

    inverse = (
        partial_table(2 ** (total_bits - low_bits), low_bits, total_bits)[:, None]
        + partial_table(2**low_bits, 0, low_bits)[None, :]
    ).reshape(-1)
    columns = jnp.arange(2**width_bits, dtype=jnp.int32)
    col_part = jnp.zeros((2**width_bits,), jnp.int32)
    for slot_no in range(width_bits):
        col_part = col_part + jnp.left_shift(
            jnp.bitwise_and(jnp.right_shift(columns, width_bits - 1 - slot_no), 1),
            chosen_bits[slot_no],
        )
    row_ids = jnp.arange(2 ** (total_bits - width_bits), dtype=jnp.int32)
    row_part = jnp.zeros((2 ** (total_bits - width_bits),), jnp.int32)
    for position in range(total_bits):
        bit_value = jnp.bitwise_and(jnp.right_shift(row_ids, free_rank[position]), 1) * 2**position
        row_part = row_part + jnp.where(chosen[position], 0, bit_value)
    gather_index = row_part[:, None] + col_part[None, :]
    return (gather_index, inverse)


def half_product(first_matrix, second_matrix):
    return jnp.dot(first_matrix, second_matrix, preferred_element_type=jnp.float32)


def merge_branch(left_factor, right_factor):
    real_part = half_product(left_factor[0], right_factor[0]) - half_product(
        left_factor[1], right_factor[1]
    )
    imag_part = half_product(left_factor[0], right_factor[1]) + half_product(
        left_factor[1], right_factor[0]
    )
    return jnp.stack([real_part, imag_part]).astype(jnp.bfloat16)


def contract_blocks(amplitude, branch, gather_index, inverse):
    lanes = 2**lane_bits
    blocks = amplitude.reshape(2, -1, lanes)
    picked = jnp.take(blocks, gather_index, axis=1)
    widened = branch.astype(jnp.float32)

    def real_product(data, matrix):
        return jnp.einsum(
            "rul,cu->rcl",
            data,
            matrix,
            precision=lax.Precision.HIGHEST,
            preferred_element_type=jnp.float32,
        )

    real_part = real_product(picked[0], widened[0]) - real_product(picked[1], widened[1])
    imag_part = real_product(picked[0], widened[1]) + real_product(picked[1], widened[0])
    merged = jnp.stack([real_part, imag_part]).reshape(2, -1, lanes)
    return jnp.take(merged, inverse, axis=1).reshape(2, -1)


def shards(stem_tensor, sub_branches, branch_bits):
    wide_count = lax.axis_size("wide")
    wide_log = wide_count.bit_length() - 1
    local_bits = LBITS
    block_shape = (2, wide_count, 2, stem_tensor.shape[1] // (2 * wide_count))
    leading = lax.axis_index("narrow") == 0

    def move_wide(amplitude):
        return lax.all_to_all(
            amplitude.reshape(block_shape), "wide", split_axis=1, concat_axis=1, tiled=True
        ).reshape(2, -1)

    def move_narrow(amplitude):
        return lax.all_to_all(
            amplitude.reshape(block_shape), "narrow", split_axis=2, concat_axis=2, tiled=True
        ).reshape(2, -1)

    def working_places(which):
        chosen_bits = branch_bits[which]
        if which == 0:
            return chosen_bits - lane_bits
        shifted = jnp.where(chosen_bits == local_bits, local_bits - wide_log - 1, chosen_bits)
        placed = jnp.where(chosen_bits > local_bits, chosen_bits - wide_log - 1, shifted)
        return placed - lane_bits

    amplitude = stem_tensor
    for which in range(BRANCHES):
        own_rows = sub_branches[which, 0]
        own_whole = lax.all_gather(own_rows, "wide", axis=1, tiled=True)
        partner_whole = partner(own_whole, "narrow", 0)
        branch = merge_branch(
            jnp.where(leading, own_whole, partner_whole),
            jnp.where(leading, partner_whole, own_whole),
        )
        if which == 1:
            amplitude = move_wide(amplitude)
        if which == 2:
            amplitude = move_narrow(amplitude)
        gather_index, inverse = bit_tables(working_places(which), local_bits - lane_bits, BBITS)
        amplitude = contract_blocks(amplitude, branch, gather_index, inverse)
    amplitude = move_narrow(amplitude)
    amplitude = move_wide(amplitude)
    return amplitude


MESH = pl.DeviceIdType.MESH


def stem_kernel(
    count, places_ref, stem_ref, sub_ref, out_ref,
    gath, bcat, work, prod, send, recv, stem_held,
    stem_sem, own_sem, z_send, z_recv, x_send, x_recv, y_send, y_recv,
    pair_send, pair_recv, swap_send, swap_recv,
):
    wide = lax.axis_index("wide")
    narrow = lax.axis_index("narrow")
    cut = lax.axis_index("cuts")
    rows = sub_ref.shape[2]
    branches = sub_ref.shape[0]
    dim = bcat.shape[1]
    total = work.shape[0]
    lanes = work.shape[1] // 2
    bits = total.bit_length() - 1
    depth = count // 2
    z = wide // 2
    x = wide % 2
    members = 2 * count
    me = wide * 2 + narrow
    piece = total // members

    stem_copy = pltpu.make_async_copy(stem_ref, stem_held, stem_sem)
    stem_copy.start()
    barrier = pltpu.get_barrier_semaphore()
    for target in ({"wide": 2 * z + 1 - x}, {"cuts": 1 - cut}, {"narrow": 1 - narrow}):
        pl.semaphore_signal(barrier, inc=1, device_id=target, device_id_type=MESH)

    @pl.when(z + 1 < depth)
    def _():
        pl.semaphore_signal(barrier, inc=1, device_id={"wide": wide + 2}, device_id_type=MESH)

    @pl.when(z > 0)
    def _():
        pl.semaphore_signal(barrier, inc=1, device_id={"wide": wide - 2}, device_id_type=MESH)

    pl.semaphore_wait(barrier, 3 + jnp.minimum(z, 1) + jnp.minimum(depth - 1 - z, 1))

    started = []
    own_copies = []

    def there(way, distance):
        return z >= distance if way == 0 else z + distance < depth

    def level(way, distance):
        return z - distance if way == 0 else z + distance

    def slot_of(way, distance):
        return 0 if distance == 0 else 1 + way * (depth - 1) + distance - 1

    def part_of(side):
        return cut if side == 0 else 1 - cut

    def copy_of(which, side, column, way, distance, send_sem, recv_sem, device_id):
        origin = 2 * level(way, distance) + (x if column == 0 else 1 - x)
        span = pl.ds(pl.multiple_of(origin * rows, rows), rows)
        target = gath.at[narrow, which, part_of(side), span]
        own = distance == 0 and column == 0
        return pltpu.make_async_remote_copy(
            src_ref=sub_ref.at[which, part_of(side)] if own else target,
            dst_ref=target,
            send_sem=send_sem,
            recv_sem=recv_sem,
            device_id=device_id,
            device_id_type=MESH,
        )

    def z_copy(which, way, distance):
        return copy_of(
            which, 0, 0, way, distance - 1,
            z_send.at[way, which, distance - 1], z_recv.at[way, which, distance - 1],
            {"wide": wide + 2 if way == 0 else wide - 2},
        )

    def x_copy(which, side, way, distance):
        slot = side if distance == 0 else 1 + slot_of(way, distance)
        return copy_of(
            which, side, 0, way, distance,
            x_send.at[which, slot], x_recv.at[which, slot], {"wide": 2 * z + 1 - x},
        )

    def y_copy(which, column, way, distance):
        slot = slot_of(way, distance)
        return copy_of(
            which, 0, column, way, distance,
            y_send.at[which, column, slot], y_recv.at[which, column, slot],
            {"cuts": 1 - cut},
        )

    def pair_copy(which, side, column, way, distance):
        slot = slot_of(way, distance)
        return copy_of(
            which, side, column, way, distance,
            pair_send.at[which, side, column, slot], pair_recv.at[which, side, column, slot],
            {"narrow": 1 - narrow},
        )

    def launch(build, guard=None):
        if guard is None:
            build().start()
        else:
            pl.when(guard)(lambda: build().start())
        started.append((build, guard))

    def finish(build, guard):
        if guard is None:
            build().wait_send()
        else:
            pl.when(guard)(lambda: build().wait_send())

    def await_recv(build, guard=None):
        if guard is None:
            build().wait_recv()
        else:
            pl.when(guard)(lambda: build().wait_recv())

    ways = (0, 1)
    part_sides = (0, 1)
    call = functools.partial

    def send_own_z(which):
        launch(call(z_copy, which, 0, 1), there(1, 1))
        launch(call(z_copy, which, 1, 1), there(0, 1))

    def send_own_x(which):
        for side in part_sides:
            launch(call(x_copy, which, side, 0, 0))
        for side in part_sides:
            launch(call(pair_copy, which, side, 0, 0, 0))
            origin = pl.ds(pl.multiple_of(wide * rows, rows), rows)
            keep = pltpu.make_async_copy(
                sub_ref.at[which, side], gath.at[narrow, which, side, origin],
                own_sem.at[which, side],
            )
            keep.start()
            own_copies.append(keep)

    def take_x_own(which):
        for side in part_sides:
            await_recv(call(x_copy, which, side, 0, 0))
            launch(call(pair_copy, which, side, 1, 0, 0))

    def take_z(which, distance):
        for way in ways:
            guard = there(way, distance)
            await_recv(call(z_copy, which, way, distance), guard)
            if distance + 1 < depth:
                launch(
                    call(z_copy, which, way, distance + 1),
                    jnp.logical_and(guard, there(1 - way, 1)),
                )
            launch(call(y_copy, which, 0, way, distance), guard)
            launch(call(x_copy, which, 0, way, distance), guard)
            launch(call(pair_copy, which, 0, 0, way, distance), guard)

    def take_x(which, distance):
        for way in ways:
            guard = there(way, distance)
            await_recv(call(x_copy, which, 0, way, distance), guard)
            launch(call(y_copy, which, 1, way, distance), guard)
            launch(call(pair_copy, which, 0, 1, way, distance), guard)

    def take_y(which, distance):
        for way in ways:
            guard = there(way, distance)
            for column in (0, 1):
                await_recv(call(y_copy, which, column, way, distance), guard)
                launch(call(pair_copy, which, 1, column, way, distance), guard)

    def complete(which):
        for side in part_sides:
            own_copies[2 * which + side].wait()
            for column in (0, 1):
                await_recv(call(pair_copy, which, side, column, 0, 0))
                for way in ways:
                    for distance in range(1, depth):
                        await_recv(
                            call(pair_copy, which, side, column, way, distance),
                            there(way, distance),
                        )

    def advance(slot):
        for which in range(branches):
            distance = slot - which
            if 1 <= distance < depth:
                take_z(which, distance)
            if 1 <= distance - 1 < depth:
                take_x(which, distance - 1)
            if distance == 2:
                take_x_own(which)
                if which + 1 < branches:
                    send_own_x(which + 1)
            if which == 0 and 1 <= distance - 2 < depth:
                take_y(which, distance - 2)

    def take_mates(which):
        for distance in range(1, depth):
            take_y(which, distance)
        complete(which)

    def merge(which):
        held = bcat.at[which % 2]
        first = [gath[0, which, part] for part in range(2)]
        second = [gath[1, which, part] for part in range(2)]

        def half_product(left, right):
            return jnp.dot(left, right, preferred_element_type=jnp.float32)

        held[:, :dim] = (
            half_product(first[0], second[0]) - half_product(first[1], second[1])
        ).astype(jnp.bfloat16)
        held[:, dim:] = (
            half_product(first[0], second[1]) + half_product(first[1], second[0])
        ).astype(jnp.bfloat16)

    width = dim.bit_length() - 1

    narrow_place = bits - 1 - (count.bit_length() - 1)

    def named_place(which, slot):
        bit = places_ref[which, slot]
        return bit + jnp.where(bit < LBITS, -lane_bits, narrow_place - LBITS)

    places = [[named_place(which, slot) for slot in range(width)] for which in range(branches)]

    def free_place(which):
        rest = bits * (bits - 1) // 2
        for slot in range(width):
            rest = rest - places[which][slot]
        return rest

    def bit_at(values, position):
        return jnp.bitwise_and(jnp.right_shift(values, position), 1)

    def gathered_place(which, values):
        found = jnp.left_shift(bit_at(values, free_place(which)), width)
        for slot in range(width):
            found = found + jnp.left_shift(
                bit_at(values, places[which][slot]), width - 1 - slot
            )
        return found

    def natural_place(which, values):
        found = jnp.left_shift(bit_at(values, width), free_place(which))
        for slot in range(width):
            found = found + jnp.left_shift(
                bit_at(values, width - 1 - slot), places[which][slot]
            )
        return found

    def permute(source, target_ref, goal):
        step = min(256, total)
        for first in range(0, total, step):
            index = lax.broadcasted_iota(jnp.int32, (step, total), 0) + first
            onehot = (index == goal).astype(jnp.float32).astype(jnp.bfloat16)
            target_ref[first:first + step, :] = jnp.dot(
                onehot, source, preferred_element_type=jnp.float32
            ).astype(jnp.bfloat16)

    def contract(which):
        for first in range(0, total, dim):
            data = work[first:first + dim, :]
            turned = jnp.concatenate([-data[:, lanes:], data[:, :lanes]], axis=1)
            both = jnp.concatenate([data, turned], axis=0)
            prod[first:first + dim, :] = jnp.dot(
                bcat[which % 2], both, preferred_element_type=jnp.float32
            ).astype(jnp.bfloat16)

    def swap_copy(round_no, step):
        other = (me + step) % members
        return pltpu.make_async_remote_copy(
            src_ref=send.at[round_no, pl.ds(pl.multiple_of(other * piece, piece), piece)],
            dst_ref=recv.at[round_no, pl.ds(pl.multiple_of(me * piece, piece), piece)],
            send_sem=swap_send.at[round_no, step],
            recv_sem=swap_recv.at[round_no, step],
            device_id={"wide": other // 2, "narrow": other % 2},
            device_id_type=MESH,
        )

    far_first = sorted(range(1, members), key=lambda step: -min(step, members - step))

    def swap_start(round_no):
        for step in far_first:
            launch(call(swap_copy, round_no, step))
        mine = pl.ds(pl.multiple_of(me * piece, piece), piece)
        recv[round_no, mine, :] = send[round_no, mine, :]

    def swap_wait(round_no):
        for step in far_first:
            swap_copy(round_no, step).wait_recv()

    line = lax.broadcasted_iota(jnp.int32, (1, total), 1)
    send_own_z(0)
    send_own_x(0)
    for which in range(1, branches):
        send_own_z(which)
    stem_copy.wait()
    stem = jnp.concatenate(
        [stem_held[pl.ds(part, total, stride=2), :] for part in range(2)], axis=1
    ).astype(jnp.bfloat16)
    permute(stem, work, gathered_place(0, line))
    for slot in range(1, depth + 2):
        advance(slot)
    complete(0)
    merge(0)
    contract(0)
    permute(prod[...], send.at[0], natural_place(0, line))
    swap_start(0)
    for slot in range(depth + 2, depth + branches):
        advance(slot)
    take_mates(1)
    merge(1)
    take_mates(2)
    merge(2)
    swap_wait(0)
    permute(recv[0], work, gathered_place(1, line))
    contract(1)
    permute(prod[...], work, gathered_place(2, natural_place(1, line)))
    contract(2)
    permute(prod[...], send.at[1], natural_place(2, line))
    swap_start(1)
    swap_wait(1)
    for part in range(2):
        out_ref[pl.ds(part, total, stride=2), :] = recv[
            1, :, part * lanes:(part + 1) * lanes
        ].astype(jnp.float32)
    for build, guard in started:
        finish(build, guard)


def shards_in_kernel(stem_tensor, sub_branches, branch_bits):
    count = lax.axis_size("wide")
    depth = count // 2
    lanes = 2**lane_bits
    total = stem_tensor.shape[1] // lanes
    dim = sub_branches.shape[-1]
    stem = stem_tensor.reshape(2, total, lanes).transpose(1, 0, 2).reshape(2 * total, lanes)
    vmem = pl.BlockSpec(memory_space=pltpu.VMEM)
    hbm = pl.BlockSpec(memory_space=pl.ANY)
    slots = 2 * depth - 1
    semaphores = [(BRANCHES, 2)]
    for shape in ((2, BRANCHES, depth), (BRANCHES, slots + 1), (BRANCHES, 2, slots),
                  (BRANCHES, 2, 2, slots), (2, 2 * count)):
        semaphores += [shape, shape]
    result = pl.pallas_call(
        functools.partial(stem_kernel, count),
        out_shape=jax.ShapeDtypeStruct((2 * total, lanes), jnp.float32),
        in_specs=[pl.BlockSpec(memory_space=pltpu.SMEM), hbm, hbm],
        out_specs=vmem,
        scratch_shapes=[
            pltpu.VMEM((2, BRANCHES, 2, dim, dim), jnp.bfloat16),
            pltpu.VMEM((2, dim, 2 * dim), jnp.bfloat16),
            pltpu.VMEM((total, 2 * lanes), jnp.bfloat16),
            pltpu.VMEM((total, 2 * lanes), jnp.bfloat16),
            pltpu.VMEM((2, total, 2 * lanes), jnp.bfloat16),
            pltpu.VMEM((2, total, 2 * lanes), jnp.bfloat16),
            pltpu.VMEM((2 * total, lanes), jnp.float32),
            pltpu.SemaphoreType.DMA(()),
        ] + [pltpu.SemaphoreType.DMA(shape) for shape in semaphores],
        compiler_params=pltpu.CompilerParams(collective_id=0, has_side_effects=True),
    )(branch_bits, stem, sub_branches[:, 0])
    return result.reshape(total, 2, lanes).transpose(1, 0, 2).reshape(2, -1)


sublane_tile = 16


def solution(mesh):
    in_specs = (P(None, ("cuts", "wide", "narrow")), P(None, "narrow", None, "wide", None), P())
    out_specs = P(None, ("cuts", "wide", "narrow"))

    def run(stem_tensor, sub_branches, branch_bits):
        whole_tiles = sub_branches.shape[3] % sublane_tile == 0 and mesh.shape["cuts"] == 2
        body = shards_in_kernel if whole_tiles else shards
        return body(stem_tensor, sub_branches, branch_bits)

    return jax.shard_map(run, mesh=mesh, in_specs=in_specs, out_specs=out_specs, check_vma=False)
```

```python
import functools

import jax
import jax.numpy as jnp
from jax import lax
from jax.experimental import pallas as pl
from jax.experimental.pallas import tpu as pltpu
from jax.sharding import PartitionSpec as P

LBITS = 17
BBITS = 9
BRANCHES = 3


lane_bits = 7


def partner(value, axis, stride):
    mask = 2**stride
    pairs = [(source, source ^ mask) for source in range(lax.axis_size(axis))]
    return lax.ppermute(value, axis, pairs)


def bit_tables(chosen_bits, total_bits, width_bits):
    places = jnp.arange(total_bits, dtype=jnp.int32)
    orders = jnp.arange(width_bits, dtype=jnp.int32)
    matches = places[:, None] == chosen_bits[None, :]
    chosen = jnp.any(matches, axis=1)
    ranking = jnp.sum(jnp.where(matches, orders[None, :], 0), axis=1)
    unchosen = 1 - chosen.astype(jnp.int32)
    free_rank = jnp.cumsum(unchosen) - unchosen
    unit_ones = jnp.ones((total_bits,), jnp.int32)
    weight = jnp.where(
        chosen,
        jnp.left_shift(unit_ones, width_bits - 1 - ranking),
        jnp.left_shift(unit_ones, width_bits + free_rank),
    )
    low_bits = total_bits // 2

    def partial_table(count, first_place, last_place):
        values = jnp.arange(count, dtype=jnp.int32)
        running = jnp.zeros((count,), jnp.int32)
        for position in range(first_place, last_place):
            running = (
                running
                + jnp.bitwise_and(jnp.right_shift(values, position - first_place), 1)
                * weight[position]
            )
        return running

    inverse = (
        partial_table(2 ** (total_bits - low_bits), low_bits, total_bits)[:, None]
        + partial_table(2**low_bits, 0, low_bits)[None, :]
    ).reshape(-1)
    columns = jnp.arange(2**width_bits, dtype=jnp.int32)
    col_part = jnp.zeros((2**width_bits,), jnp.int32)
    for slot_no in range(width_bits):
        col_part = col_part + jnp.left_shift(
            jnp.bitwise_and(jnp.right_shift(columns, width_bits - 1 - slot_no), 1),
            chosen_bits[slot_no],
        )
    row_ids = jnp.arange(2 ** (total_bits - width_bits), dtype=jnp.int32)
    row_part = jnp.zeros((2 ** (total_bits - width_bits),), jnp.int32)
    for position in range(total_bits):
        bit_value = jnp.bitwise_and(jnp.right_shift(row_ids, free_rank[position]), 1) * 2**position
        row_part = row_part + jnp.where(chosen[position], 0, bit_value)
    gather_index = row_part[:, None] + col_part[None, :]
    return (gather_index, inverse)


def half_product(first_matrix, second_matrix):
    return jnp.dot(first_matrix, second_matrix, preferred_element_type=jnp.float32)


def merge_branch(left_factor, right_factor):
    real_part = half_product(left_factor[0], right_factor[0]) - half_product(
        left_factor[1], right_factor[1]
    )
    imag_part = half_product(left_factor[0], right_factor[1]) + half_product(
        left_factor[1], right_factor[0]
    )
    return jnp.stack([real_part, imag_part]).astype(jnp.bfloat16)


def contract_blocks(amplitude, branch, gather_index, inverse):
    lanes = 2**lane_bits
    blocks = amplitude.reshape(2, -1, lanes)
    picked = jnp.take(blocks, gather_index, axis=1)
    widened = branch.astype(jnp.float32)

    def real_product(data, matrix):
        return jnp.einsum(
            "rul,cu->rcl",
            data,
            matrix,
            precision=lax.Precision.HIGHEST,
            preferred_element_type=jnp.float32,
        )

    real_part = real_product(picked[0], widened[0]) - real_product(picked[1], widened[1])
    imag_part = real_product(picked[0], widened[1]) + real_product(picked[1], widened[0])
    merged = jnp.stack([real_part, imag_part]).reshape(2, -1, lanes)
    return jnp.take(merged, inverse, axis=1).reshape(2, -1)


def shards(stem_tensor, sub_branches, branch_bits):
    wide_count = lax.axis_size("wide")
    wide_log = wide_count.bit_length() - 1
    local_bits = LBITS
    block_shape = (2, wide_count, 2, stem_tensor.shape[1] // (2 * wide_count))
    leading = lax.axis_index("narrow") == 0

    def move_wide(amplitude):
        return lax.all_to_all(
            amplitude.reshape(block_shape), "wide", split_axis=1, concat_axis=1, tiled=True
        ).reshape(2, -1)

    def move_narrow(amplitude):
        return lax.all_to_all(
            amplitude.reshape(block_shape), "narrow", split_axis=2, concat_axis=2, tiled=True
        ).reshape(2, -1)

    def working_places(which):
        chosen_bits = branch_bits[which]
        if which == 0:
            return chosen_bits - lane_bits
        shifted = jnp.where(chosen_bits == local_bits, local_bits - wide_log - 1, chosen_bits)
        placed = jnp.where(chosen_bits > local_bits, chosen_bits - wide_log - 1, shifted)
        return placed - lane_bits

    amplitude = stem_tensor
    for which in range(BRANCHES):
        own_rows = sub_branches[which, 0]
        own_whole = lax.all_gather(own_rows, "wide", axis=1, tiled=True)
        partner_whole = partner(own_whole, "narrow", 0)
        branch = merge_branch(
            jnp.where(leading, own_whole, partner_whole),
            jnp.where(leading, partner_whole, own_whole),
        )
        if which == 1:
            amplitude = move_wide(amplitude)
        if which == 2:
            amplitude = move_narrow(amplitude)
        gather_index, inverse = bit_tables(working_places(which), local_bits - lane_bits, BBITS)
        amplitude = contract_blocks(amplitude, branch, gather_index, inverse)
    amplitude = move_narrow(amplitude)
    amplitude = move_wide(amplitude)
    return amplitude


MESH = pl.DeviceIdType.MESH


def stem_kernel(
    count, places_ref, stem_ref, sub_ref, out_ref,
    gath, bcat, work, prod, send, recv, stem_held,
    stem_sem, own_sem, z_send, z_recv, x_send, x_recv, y_send, y_recv,
    pair_send, pair_recv, swap_send, swap_recv,
):
    wide = lax.axis_index("wide")
    narrow = lax.axis_index("narrow")
    cut = lax.axis_index("cuts")
    rows = sub_ref.shape[2]
    branches = sub_ref.shape[0]
    dim = bcat.shape[1]
    total = work.shape[0]
    lanes = work.shape[1] // 2
    bits = total.bit_length() - 1
    depth = count // 2
    z = wide // 2
    x = wide % 2
    members = 2 * count
    me = wide * 2 + narrow
    piece = total // members

    stem_copy = pltpu.make_async_copy(stem_ref, stem_held, stem_sem)
    stem_copy.start()
    barrier = pltpu.get_barrier_semaphore()
    for target in ({"wide": 2 * z + 1 - x}, {"cuts": 1 - cut}, {"narrow": 1 - narrow}):
        pl.semaphore_signal(barrier, inc=1, device_id=target, device_id_type=MESH)

    @pl.when(z + 1 < depth)
    def _():
        pl.semaphore_signal(barrier, inc=1, device_id={"wide": wide + 2}, device_id_type=MESH)

    @pl.when(z > 0)
    def _():
        pl.semaphore_signal(barrier, inc=1, device_id={"wide": wide - 2}, device_id_type=MESH)

    pl.semaphore_wait(barrier, 3 + jnp.minimum(z, 1) + jnp.minimum(depth - 1 - z, 1))

    started = []
    own_copies = []

    def there(way, distance):
        return z >= distance if way == 0 else z + distance < depth

    def level(way, distance):
        return z - distance if way == 0 else z + distance

    def slot_of(way, distance):
        return 0 if distance == 0 else 1 + way * (depth - 1) + distance - 1

    def part_of(side):
        return cut if side == 0 else 1 - cut

    def copy_of(which, side, column, way, distance, send_sem, recv_sem, device_id):
        origin = 2 * level(way, distance) + (x if column == 0 else 1 - x)
        span = pl.ds(pl.multiple_of(origin * rows, rows), rows)
        target = gath.at[narrow, which, part_of(side), span]
        own = distance == 0 and column == 0
        return pltpu.make_async_remote_copy(
            src_ref=sub_ref.at[which, part_of(side)] if own else target,
            dst_ref=target,
            send_sem=send_sem,
            recv_sem=recv_sem,
            device_id=device_id,
            device_id_type=MESH,
        )

    def z_copy(which, side, way, distance):
        slot = depth - 1 if side == 1 else distance - 1
        return copy_of(
            which, side, 0, way, distance - 1,
            z_send.at[way, which, slot], z_recv.at[way, which, slot],
            {"wide": wide + 2 if way == 0 else wide - 2},
        )

    def x_copy(which, side, way, distance):
        slot = side if distance == 0 else 1 + slot_of(way, distance)
        return copy_of(
            which, side, 0, way, distance,
            x_send.at[which, slot], x_recv.at[which, slot], {"wide": 2 * z + 1 - x},
        )

    def y_copy(which, column, way, distance):
        slot = slot_of(way, distance)
        return copy_of(
            which, 0, column, way, distance,
            y_send.at[which, column, slot], y_recv.at[which, column, slot],
            {"cuts": 1 - cut},
        )

    def pair_copy(which, side, column, way, distance):
        slot = slot_of(way, distance)
        return copy_of(
            which, side, column, way, distance,
            pair_send.at[which, side, column, slot], pair_recv.at[which, side, column, slot],
            {"narrow": 1 - narrow},
        )

    def launch(build, guard=None):
        if guard is None:
            build().start()
        else:
            pl.when(guard)(lambda: build().start())
        started.append((build, guard))

    def finish(build, guard):
        if guard is None:
            build().wait_send()
        else:
            pl.when(guard)(lambda: build().wait_send())

    def await_recv(build, guard=None):
        if guard is None:
            build().wait_recv()
        else:
            pl.when(guard)(lambda: build().wait_recv())

    ways = (0, 1)
    part_sides = (0, 1)
    call = functools.partial

    def send_own_z(which):
        for side in part_sides:
            for way in ways:
                launch(call(z_copy, which, side, way, 1), there(1 - way, 1))

    def send_own_x(which):
        for side in part_sides:
            launch(call(x_copy, which, side, 0, 0))
        for side in part_sides:
            launch(call(pair_copy, which, side, 0, 0, 0))
            origin = pl.ds(pl.multiple_of(wide * rows, rows), rows)
            keep = pltpu.make_async_copy(
                sub_ref.at[which, side], gath.at[narrow, which, side, origin],
                own_sem.at[which, side],
            )
            keep.start()
            own_copies.append(keep)

    def take_x_own(which):
        for side in part_sides:
            await_recv(call(x_copy, which, side, 0, 0))
            launch(call(pair_copy, which, side, 1, 0, 0))

    def take_z(which, distance):
        for way in ways:
            guard = there(way, distance)
            await_recv(call(z_copy, which, 0, way, distance), guard)
            if distance + 1 < depth:
                launch(
                    call(z_copy, which, 0, way, distance + 1),
                    jnp.logical_and(guard, there(1 - way, 1)),
                )
            if distance > 1:
                launch(call(y_copy, which, 0, way, distance), guard)
            launch(call(x_copy, which, 0, way, distance), guard)
            launch(call(pair_copy, which, 0, 0, way, distance), guard)

    def take_x(which, distance):
        for way in ways:
            guard = there(way, distance)
            await_recv(call(x_copy, which, 0, way, distance), guard)
            launch(call(y_copy, which, 1, way, distance), guard)
            launch(call(pair_copy, which, 0, 1, way, distance), guard)

    def take_y(which, distance):
        for way in ways:
            guard = there(way, distance)
            for column in (0, 1):
                if column == 0 and distance == 1:
                    await_recv(call(z_copy, which, 1, way, 1), guard)
                else:
                    await_recv(call(y_copy, which, column, way, distance), guard)
                launch(call(pair_copy, which, 1, column, way, distance), guard)

    def complete(which):
        for side in part_sides:
            own_copies[2 * which + side].wait()
            for column in (0, 1):
                await_recv(call(pair_copy, which, side, column, 0, 0))
                for way in ways:
                    for distance in range(1, depth):
                        await_recv(
                            call(pair_copy, which, side, column, way, distance),
                            there(way, distance),
                        )

    def advance(slot):
        for which in range(branches):
            distance = slot - which
            if 1 <= distance < depth:
                take_z(which, distance)
            if 1 <= distance - 1 < depth:
                take_x(which, distance - 1)
            if distance == 2:
                take_x_own(which)
                if which + 1 < branches:
                    send_own_x(which + 1)
            if which == 0 and 1 <= distance - 2 < depth:
                take_y(which, distance - 2)

    def take_mates(which):
        for distance in range(1, depth):
            take_y(which, distance)

    def merge(which):
        held = bcat.at[which % 2]
        first = [gath[0, which, part] for part in range(2)]
        second = [gath[1, which, part] for part in range(2)]

        def half_product(left, right):
            return jnp.dot(left, right, preferred_element_type=jnp.float32)

        held[:, :dim] = (
            half_product(first[0], second[0]) - half_product(first[1], second[1])
        ).astype(jnp.bfloat16)
        held[:, dim:] = (
            half_product(first[0], second[1]) + half_product(first[1], second[0])
        ).astype(jnp.bfloat16)

    width = dim.bit_length() - 1

    narrow_place = bits - 1 - (count.bit_length() - 1)

    def named_place(which, slot):
        bit = places_ref[which, slot]
        return bit + jnp.where(bit < LBITS, -lane_bits, narrow_place - LBITS)

    places = [[named_place(which, slot) for slot in range(width)] for which in range(branches)]

    def free_place(which):
        rest = bits * (bits - 1) // 2
        for slot in range(width):
            rest = rest - places[which][slot]
        return rest

    def bit_at(values, position):
        return jnp.bitwise_and(jnp.right_shift(values, position), 1)

    def gathered_place(which, values):
        found = jnp.left_shift(bit_at(values, free_place(which)), width)
        for slot in range(width):
            found = found + jnp.left_shift(
                bit_at(values, places[which][slot]), width - 1 - slot
            )
        return found

    def natural_place(which, values):
        found = jnp.left_shift(bit_at(values, width), free_place(which))
        for slot in range(width):
            found = found + jnp.left_shift(
                bit_at(values, width - 1 - slot), places[which][slot]
            )
        return found

    def permute(source, target_ref, goal):
        step = min(256, total)
        for first in range(0, total, step):
            index = lax.broadcasted_iota(jnp.int32, (step, total), 0) + first
            onehot = (index == goal).astype(jnp.float32).astype(jnp.bfloat16)
            target_ref[first:first + step, :] = jnp.dot(
                onehot, source, preferred_element_type=jnp.float32
            ).astype(jnp.bfloat16)

    def contract(which):
        for first in range(0, total, dim):
            data = work[first:first + dim, :]
            turned = jnp.concatenate([-data[:, lanes:], data[:, :lanes]], axis=1)
            both = jnp.concatenate([data, turned], axis=0)
            prod[first:first + dim, :] = jnp.dot(
                bcat[which % 2], both, preferred_element_type=jnp.float32
            ).astype(jnp.bfloat16)

    far_first = sorted(range(depth), key=lambda hop: -min(hop, depth - hop))
    level_rows = total // depth

    def swap_targets(round_no, hop):
        level_z = (z + hop) % depth
        for turn in range(4):
            across, other_core = turn // 2, turn % 2
            if hop == 0 and turn == 0:
                continue
            to_x = x if across == 0 else 1 - x
            to_core = narrow if other_core == 0 else 1 - narrow
            to_wide = 2 * level_z + to_x
            other = 2 * to_wide + to_core
            yield pltpu.make_async_remote_copy(
                src_ref=send.at[round_no, pl.ds(pl.multiple_of(other * piece, piece), piece)],
                dst_ref=recv.at[round_no, pl.ds(pl.multiple_of(me * piece, piece), piece)],
                send_sem=swap_send.at[round_no, 4 * hop + turn],
                recv_sem=swap_recv.at[round_no, 4 * hop + turn],
                device_id={"wide": to_wide, "narrow": to_core},
                device_id_type=MESH,
            )

    def swap_level(round_no, hop, source, goal):
        first = ((z + hop) % depth) * level_rows
        index = lax.broadcasted_iota(jnp.int32, (level_rows, total), 0) + first
        onehot = (index == goal).astype(jnp.float32).astype(jnp.bfloat16)
        send[round_no, pl.ds(pl.multiple_of(first, level_rows), level_rows), :] = jnp.dot(
            onehot, source, preferred_element_type=jnp.float32
        ).astype(jnp.bfloat16)
        for copy in swap_targets(round_no, hop):
            copy.start()

    def swap_out(round_no, goal):
        source = prod[...]
        for hop in far_first:
            swap_level(round_no, hop, source, goal)
        mine = pl.ds(pl.multiple_of(me * piece, piece), piece)
        recv[round_no, mine, :] = send[round_no, mine, :]

    def swap_wait(round_no):
        for hop in far_first:
            for copy in swap_targets(round_no, hop):
                copy.wait_recv()

    line = lax.broadcasted_iota(jnp.int32, (1, total), 1)
    send_own_z(0)
    send_own_x(0)
    for which in range(1, branches):
        send_own_z(which)
    stem_copy.wait()
    stem = jnp.concatenate(
        [stem_held[pl.ds(part, total, stride=2), :] for part in range(2)], axis=1
    ).astype(jnp.bfloat16)
    permute(stem, work, gathered_place(0, line))
    for slot in range(1, depth + 2):
        advance(slot)
    complete(0)
    merge(0)
    contract(0)
    swap_out(0, natural_place(0, line))
    for slot in range(depth + 2, depth + branches):
        advance(slot)
    take_mates(1)
    complete(1)
    merge(1)
    take_mates(2)
    swap_wait(0)
    permute(recv[0], work, gathered_place(1, line))
    contract(1)
    permute(prod[...], work, gathered_place(2, natural_place(1, line)))
    complete(2)
    merge(2)
    contract(2)
    swap_out(1, natural_place(2, line))
    swap_wait(1)
    for part in range(2):
        out_ref[pl.ds(part, total, stride=2), :] = recv[
            1, :, part * lanes:(part + 1) * lanes
        ].astype(jnp.float32)
    for round_no in range(2):
        for hop in range(depth):
            for copy in swap_targets(round_no, hop):
                copy.wait_send()
    for build, guard in started:
        finish(build, guard)


def shards_in_kernel(stem_tensor, sub_branches, branch_bits):
    count = lax.axis_size("wide")
    depth = count // 2
    lanes = 2**lane_bits
    total = stem_tensor.shape[1] // lanes
    dim = sub_branches.shape[-1]
    stem = stem_tensor.reshape(2, total, lanes).transpose(1, 0, 2).reshape(2 * total, lanes)
    vmem = pl.BlockSpec(memory_space=pltpu.VMEM)
    hbm = pl.BlockSpec(memory_space=pl.ANY)
    slots = 2 * depth - 1
    semaphores = [(BRANCHES, 2)]
    for shape in ((2, BRANCHES, depth), (BRANCHES, slots + 1), (BRANCHES, 2, slots),
                  (BRANCHES, 2, 2, slots), (2, 2 * count)):
        semaphores += [shape, shape]
    result = pl.pallas_call(
        functools.partial(stem_kernel, count),
        out_shape=jax.ShapeDtypeStruct((2 * total, lanes), jnp.float32),
        in_specs=[pl.BlockSpec(memory_space=pltpu.SMEM), hbm, hbm],
        out_specs=vmem,
        scratch_shapes=[
            pltpu.VMEM((2, BRANCHES, 2, dim, dim), jnp.bfloat16),
            pltpu.VMEM((2, dim, 2 * dim), jnp.bfloat16),
            pltpu.VMEM((total, 2 * lanes), jnp.bfloat16),
            pltpu.VMEM((total, 2 * lanes), jnp.bfloat16),
            pltpu.VMEM((2, total, 2 * lanes), jnp.bfloat16),
            pltpu.VMEM((2, total, 2 * lanes), jnp.bfloat16),
            pltpu.VMEM((2 * total, lanes), jnp.float32),
            pltpu.SemaphoreType.DMA(()),
        ] + [pltpu.SemaphoreType.DMA(shape) for shape in semaphores],
        compiler_params=pltpu.CompilerParams(collective_id=0, has_side_effects=True),
    )(branch_bits, stem, sub_branches[:, 0])
    return result.reshape(total, 2, lanes).transpose(1, 0, 2).reshape(2, -1)


sublane_tile = 16


def solution(mesh):
    in_specs = (P(None, ("cuts", "wide", "narrow")), P(None, "narrow", None, "wide", None), P())
    out_specs = P(None, ("cuts", "wide", "narrow"))

    def run(stem_tensor, sub_branches, branch_bits):
        whole_tiles = sub_branches.shape[3] % sublane_tile == 0 and mesh.shape["cuts"] == 2
        body = shards_in_kernel if whole_tiles else shards
        return body(stem_tensor, sub_branches, branch_bits)

    return jax.shard_map(run, mesh=mesh, in_specs=in_specs, out_specs=out_specs, check_vma=False)
```

```python
import functools

import jax
import jax.numpy as jnp
from jax import lax
from jax.experimental import pallas as pl
from jax.experimental.pallas import tpu as pltpu
from jax.sharding import PartitionSpec as P

LBITS = 17
BBITS = 9
BRANCHES = 3


lane_bits = 7


def partner(value, axis, stride):
    mask = 2**stride
    pairs = [(source, source ^ mask) for source in range(lax.axis_size(axis))]
    return lax.ppermute(value, axis, pairs)


def bit_tables(chosen_bits, total_bits, width_bits):
    places = jnp.arange(total_bits, dtype=jnp.int32)
    orders = jnp.arange(width_bits, dtype=jnp.int32)
    matches = places[:, None] == chosen_bits[None, :]
    chosen = jnp.any(matches, axis=1)
    ranking = jnp.sum(jnp.where(matches, orders[None, :], 0), axis=1)
    unchosen = 1 - chosen.astype(jnp.int32)
    free_rank = jnp.cumsum(unchosen) - unchosen
    unit_ones = jnp.ones((total_bits,), jnp.int32)
    weight = jnp.where(
        chosen,
        jnp.left_shift(unit_ones, width_bits - 1 - ranking),
        jnp.left_shift(unit_ones, width_bits + free_rank),
    )
    low_bits = total_bits // 2

    def partial_table(count, first_place, last_place):
        values = jnp.arange(count, dtype=jnp.int32)
        running = jnp.zeros((count,), jnp.int32)
        for position in range(first_place, last_place):
            running = (
                running
                + jnp.bitwise_and(jnp.right_shift(values, position - first_place), 1)
                * weight[position]
            )
        return running

    inverse = (
        partial_table(2 ** (total_bits - low_bits), low_bits, total_bits)[:, None]
        + partial_table(2**low_bits, 0, low_bits)[None, :]
    ).reshape(-1)
    columns = jnp.arange(2**width_bits, dtype=jnp.int32)
    col_part = jnp.zeros((2**width_bits,), jnp.int32)
    for slot_no in range(width_bits):
        col_part = col_part + jnp.left_shift(
            jnp.bitwise_and(jnp.right_shift(columns, width_bits - 1 - slot_no), 1),
            chosen_bits[slot_no],
        )
    row_ids = jnp.arange(2 ** (total_bits - width_bits), dtype=jnp.int32)
    row_part = jnp.zeros((2 ** (total_bits - width_bits),), jnp.int32)
    for position in range(total_bits):
        bit_value = jnp.bitwise_and(jnp.right_shift(row_ids, free_rank[position]), 1) * 2**position
        row_part = row_part + jnp.where(chosen[position], 0, bit_value)
    gather_index = row_part[:, None] + col_part[None, :]
    return (gather_index, inverse)


def half_product(first_matrix, second_matrix):
    return jnp.dot(first_matrix, second_matrix, preferred_element_type=jnp.float32)


def merge_branch(left_factor, right_factor):
    real_part = half_product(left_factor[0], right_factor[0]) - half_product(
        left_factor[1], right_factor[1]
    )
    imag_part = half_product(left_factor[0], right_factor[1]) + half_product(
        left_factor[1], right_factor[0]
    )
    return jnp.stack([real_part, imag_part]).astype(jnp.bfloat16)


def contract_blocks(amplitude, branch, gather_index, inverse):
    lanes = 2**lane_bits
    blocks = amplitude.reshape(2, -1, lanes)
    picked = jnp.take(blocks, gather_index, axis=1)
    widened = branch.astype(jnp.float32)

    def real_product(data, matrix):
        return jnp.einsum(
            "rul,cu->rcl",
            data,
            matrix,
            precision=lax.Precision.HIGHEST,
            preferred_element_type=jnp.float32,
        )

    real_part = real_product(picked[0], widened[0]) - real_product(picked[1], widened[1])
    imag_part = real_product(picked[0], widened[1]) + real_product(picked[1], widened[0])
    merged = jnp.stack([real_part, imag_part]).reshape(2, -1, lanes)
    return jnp.take(merged, inverse, axis=1).reshape(2, -1)


def shards(stem_tensor, sub_branches, branch_bits):
    wide_count = lax.axis_size("wide")
    wide_log = wide_count.bit_length() - 1
    local_bits = LBITS
    block_shape = (2, wide_count, 2, stem_tensor.shape[1] // (2 * wide_count))
    leading = lax.axis_index("narrow") == 0

    def move_wide(amplitude):
        return lax.all_to_all(
            amplitude.reshape(block_shape), "wide", split_axis=1, concat_axis=1, tiled=True
        ).reshape(2, -1)

    def move_narrow(amplitude):
        return lax.all_to_all(
            amplitude.reshape(block_shape), "narrow", split_axis=2, concat_axis=2, tiled=True
        ).reshape(2, -1)

    def working_places(which):
        chosen_bits = branch_bits[which]
        if which == 0:
            return chosen_bits - lane_bits
        shifted = jnp.where(chosen_bits == local_bits, local_bits - wide_log - 1, chosen_bits)
        placed = jnp.where(chosen_bits > local_bits, chosen_bits - wide_log - 1, shifted)
        return placed - lane_bits

    amplitude = stem_tensor
    for which in range(BRANCHES):
        own_rows = sub_branches[which, 0]
        own_whole = lax.all_gather(own_rows, "wide", axis=1, tiled=True)
        partner_whole = partner(own_whole, "narrow", 0)
        branch = merge_branch(
            jnp.where(leading, own_whole, partner_whole),
            jnp.where(leading, partner_whole, own_whole),
        )
        if which == 1:
            amplitude = move_wide(amplitude)
        if which == 2:
            amplitude = move_narrow(amplitude)
        gather_index, inverse = bit_tables(working_places(which), local_bits - lane_bits, BBITS)
        amplitude = contract_blocks(amplitude, branch, gather_index, inverse)
    amplitude = move_narrow(amplitude)
    amplitude = move_wide(amplitude)
    return amplitude


MESH = pl.DeviceIdType.MESH


def stem_kernel(
    count, places_ref, stem_ref, sub_ref, out_ref,
    gath, bcat, work, prod, send, recv, stem_held,
    stem_sem, own_sem, z_send, z_recv, x_send, x_recv, y_send, y_recv,
    pair_send, pair_recv, swap_send, swap_recv,
):
    wide = lax.axis_index("wide")
    narrow = lax.axis_index("narrow")
    cut = lax.axis_index("cuts")
    rows = sub_ref.shape[2]
    branches = sub_ref.shape[0]
    dim = bcat.shape[1]
    total = work.shape[0]
    lanes = work.shape[1] // 2
    bits = total.bit_length() - 1
    depth = count // 2
    z = wide // 2
    x = wide % 2
    members = 2 * count
    me = wide * 2 + narrow
    piece = total // members

    stem_copy = pltpu.make_async_copy(stem_ref, stem_held, stem_sem)
    stem_copy.start()
    barrier = pltpu.get_barrier_semaphore()
    for target in ({"wide": 2 * z + 1 - x}, {"cuts": 1 - cut}, {"narrow": 1 - narrow}):
        pl.semaphore_signal(barrier, inc=1, device_id=target, device_id_type=MESH)

    @pl.when(z + 1 < depth)
    def _():
        pl.semaphore_signal(barrier, inc=1, device_id={"wide": wide + 2}, device_id_type=MESH)

    @pl.when(z > 0)
    def _():
        pl.semaphore_signal(barrier, inc=1, device_id={"wide": wide - 2}, device_id_type=MESH)

    pl.semaphore_wait(barrier, 3 + jnp.minimum(z, 1) + jnp.minimum(depth - 1 - z, 1))

    started = []
    own_copies = []

    def there(way, distance):
        return z >= distance if way == 0 else z + distance < depth

    def level(way, distance):
        return z - distance if way == 0 else z + distance

    def slot_of(way, distance):
        return 0 if distance == 0 else 1 + way * (depth - 1) + distance - 1

    def part_of(side):
        return cut if side == 0 else 1 - cut

    def copy_of(which, side, column, way, distance, send_sem, recv_sem, device_id):
        origin = 2 * level(way, distance) + (x if column == 0 else 1 - x)
        span = pl.ds(pl.multiple_of(origin * rows, rows), rows)
        target = gath.at[narrow, which, part_of(side), span]
        own = distance == 0 and column == 0
        return pltpu.make_async_remote_copy(
            src_ref=sub_ref.at[which, part_of(side)] if own else target,
            dst_ref=target,
            send_sem=send_sem,
            recv_sem=recv_sem,
            device_id=device_id,
            device_id_type=MESH,
        )

    def z_copy(which, side, way, distance):
        slot = depth - 1 if side == 1 else distance - 1
        return copy_of(
            which, side, 0, way, distance - 1,
            z_send.at[way, which, slot], z_recv.at[way, which, slot],
            {"wide": wide + 2 if way == 0 else wide - 2},
        )

    def x_copy(which, side, way, distance):
        slot = side if distance == 0 else 1 + slot_of(way, distance)
        return copy_of(
            which, side, 0, way, distance,
            x_send.at[which, slot], x_recv.at[which, slot], {"wide": 2 * z + 1 - x},
        )

    def y_copy(which, column, way, distance):
        slot = slot_of(way, distance)
        return copy_of(
            which, 0, column, way, distance,
            y_send.at[which, column, slot], y_recv.at[which, column, slot],
            {"cuts": 1 - cut},
        )

    def pair_copy(which, side, column, way, distance):
        slot = slot_of(way, distance)
        return copy_of(
            which, side, column, way, distance,
            pair_send.at[which, side, column, slot], pair_recv.at[which, side, column, slot],
            {"narrow": 1 - narrow},
        )

    def launch(build, guard=None):
        if guard is None:
            build().start()
        else:
            pl.when(guard)(lambda: build().start())
        started.append((build, guard))

    def finish(build, guard):
        if guard is None:
            build().wait_send()
        else:
            pl.when(guard)(lambda: build().wait_send())

    def await_recv(build, guard=None):
        if guard is None:
            build().wait_recv()
        else:
            pl.when(guard)(lambda: build().wait_recv())

    ways = (0, 1)
    part_sides = (0, 1)
    call = functools.partial

    def send_own_z(which):
        for way in ways:
            launch(call(z_copy, which, 0, way, 1), there(1 - way, 1))

    def send_own_x(which):
        for side in part_sides:
            launch(call(x_copy, which, side, 0, 0))
        for side in part_sides:
            launch(call(pair_copy, which, side, 0, 0, 0))
            origin = pl.ds(pl.multiple_of(wide * rows, rows), rows)
            keep = pltpu.make_async_copy(
                sub_ref.at[which, side], gath.at[narrow, which, side, origin],
                own_sem.at[which, side],
            )
            keep.start()
            own_copies.append(keep)

    def take_x_own(which):
        for side in part_sides:
            await_recv(call(x_copy, which, side, 0, 0))
            launch(call(pair_copy, which, side, 1, 0, 0))

    def take_z(which, distance):
        for way in ways:
            guard = there(way, distance)
            await_recv(call(z_copy, which, 0, way, distance), guard)
            if distance + 1 < depth:
                launch(
                    call(z_copy, which, 0, way, distance + 1),
                    jnp.logical_and(guard, there(1 - way, 1)),
                )
            launch(call(y_copy, which, 0, way, distance), guard)
            launch(call(x_copy, which, 0, way, distance), guard)
            launch(call(pair_copy, which, 0, 0, way, distance), guard)

    def take_x(which, distance):
        for way in ways:
            guard = there(way, distance)
            await_recv(call(x_copy, which, 0, way, distance), guard)
            launch(call(y_copy, which, 1, way, distance), guard)
            launch(call(pair_copy, which, 0, 1, way, distance), guard)

    def take_y(which, distance):
        for way in ways:
            guard = there(way, distance)
            for column in (0, 1):
                await_recv(call(y_copy, which, column, way, distance), guard)
                launch(call(pair_copy, which, 1, column, way, distance), guard)

    def complete(which):
        for side in part_sides:
            own_copies[2 * which + side].wait()
            for column in (0, 1):
                await_recv(call(pair_copy, which, side, column, 0, 0))
                for way in ways:
                    for distance in range(1, depth):
                        await_recv(
                            call(pair_copy, which, side, column, way, distance),
                            there(way, distance),
                        )

    def advance(slot):
        for which in range(branches):
            distance = slot - which
            if 1 <= distance < depth:
                take_z(which, distance)
            if distance == 1 and which + 1 < branches:
                send_own_z(which + 1)
            if 1 <= distance - 1 < depth:
                take_x(which, distance - 1)
            if distance == 2:
                take_x_own(which)
                if which + 1 < branches:
                    send_own_x(which + 1)
            if which == 0 and 1 <= distance - 2 < depth:
                take_y(which, distance - 2)

    def take_mates(which):
        for distance in range(1, depth):
            take_y(which, distance)

    def merge(which):
        held = bcat.at[which % 2]
        first = [gath[0, which, part] for part in range(2)]
        second = [gath[1, which, part] for part in range(2)]

        def half_product(left, right):
            return jnp.dot(left, right, preferred_element_type=jnp.float32)

        held[:, :dim] = (
            half_product(first[0], second[0]) - half_product(first[1], second[1])
        ).astype(jnp.bfloat16)
        held[:, dim:] = (
            half_product(first[0], second[1]) + half_product(first[1], second[0])
        ).astype(jnp.bfloat16)

    width = dim.bit_length() - 1

    narrow_place = bits - 1 - (count.bit_length() - 1)

    def named_place(which, slot):
        bit = places_ref[which, slot]
        return bit + jnp.where(bit < LBITS, -lane_bits, narrow_place - LBITS)

    places = [[named_place(which, slot) for slot in range(width)] for which in range(branches)]

    def free_place(which):
        rest = bits * (bits - 1) // 2
        for slot in range(width):
            rest = rest - places[which][slot]
        return rest

    def bit_at(values, position):
        return jnp.bitwise_and(jnp.right_shift(values, position), 1)

    def gathered_place(which, values):
        found = jnp.left_shift(bit_at(values, free_place(which)), width)
        for slot in range(width):
            found = found + jnp.left_shift(
                bit_at(values, places[which][slot]), width - 1 - slot
            )
        return found

    def natural_place(which, values):
        found = jnp.left_shift(bit_at(values, width), free_place(which))
        for slot in range(width):
            found = found + jnp.left_shift(
                bit_at(values, width - 1 - slot), places[which][slot]
            )
        return found

    def permute(source, target_ref, goal):
        step = min(256, total)
        for first in range(0, total, step):
            index = lax.broadcasted_iota(jnp.int32, (step, total), 0) + first
            onehot = (index == goal).astype(jnp.float32).astype(jnp.bfloat16)
            target_ref[first:first + step, :] = jnp.dot(
                onehot, source, preferred_element_type=jnp.float32
            ).astype(jnp.bfloat16)

    def contract(which):
        for first in range(0, total, dim):
            data = work[first:first + dim, :]
            turned = jnp.concatenate([-data[:, lanes:], data[:, :lanes]], axis=1)
            both = jnp.concatenate([data, turned], axis=0)
            prod[first:first + dim, :] = jnp.dot(
                bcat[which % 2], both, preferred_element_type=jnp.float32
            ).astype(jnp.bfloat16)

    far_first = sorted(range(depth), key=lambda hop: -min(hop, depth - hop))
    level_rows = total // depth

    def swap_targets(round_no, hop):
        level_z = (z + hop) % depth
        for turn in range(4):
            across, other_core = turn // 2, turn % 2
            if hop == 0 and turn == 0:
                continue
            to_x = x if across == 0 else 1 - x
            to_core = narrow if other_core == 0 else 1 - narrow
            to_wide = 2 * level_z + to_x
            other = 2 * to_wide + to_core
            yield pltpu.make_async_remote_copy(
                src_ref=send.at[round_no, pl.ds(pl.multiple_of(other * piece, piece), piece)],
                dst_ref=recv.at[round_no, pl.ds(pl.multiple_of(me * piece, piece), piece)],
                send_sem=swap_send.at[round_no, 4 * hop + turn],
                recv_sem=swap_recv.at[round_no, 4 * hop + turn],
                device_id={"wide": to_wide, "narrow": to_core},
                device_id_type=MESH,
            )

    def swap_level(round_no, hop, source, goal):
        first = ((z + hop) % depth) * level_rows
        index = lax.broadcasted_iota(jnp.int32, (level_rows, total), 0) + first
        onehot = (index == goal).astype(jnp.float32).astype(jnp.bfloat16)
        send[round_no, pl.ds(pl.multiple_of(first, level_rows), level_rows), :] = jnp.dot(
            onehot, source, preferred_element_type=jnp.float32
        ).astype(jnp.bfloat16)
        for copy in swap_targets(round_no, hop):
            copy.start()

    def swap_out(round_no, goal):
        source = prod[...]
        for hop in far_first:
            swap_level(round_no, hop, source, goal)
        mine = pl.ds(pl.multiple_of(me * piece, piece), piece)
        recv[round_no, mine, :] = send[round_no, mine, :]

    def swap_wait(round_no):
        for hop in far_first:
            for copy in swap_targets(round_no, hop):
                copy.wait_recv()

    line = lax.broadcasted_iota(jnp.int32, (1, total), 1)
    send_own_z(0)
    send_own_x(0)
    stem_copy.wait()
    stem = jnp.concatenate(
        [stem_held[pl.ds(part, total, stride=2), :] for part in range(2)], axis=1
    ).astype(jnp.bfloat16)
    permute(stem, work, gathered_place(0, line))
    for slot in range(1, depth + 2):
        advance(slot)
    complete(0)
    merge(0)
    contract(0)
    swap_out(0, natural_place(0, line))
    for slot in range(depth + 2, depth + branches):
        advance(slot)
    take_mates(1)
    complete(1)
    merge(1)
    take_mates(2)
    complete(2)
    merge(2)
    swap_wait(0)
    permute(recv[0], work, gathered_place(1, line))
    contract(1)
    permute(prod[...], work, gathered_place(2, natural_place(1, line)))
    contract(2)
    swap_out(1, natural_place(2, line))
    swap_wait(1)
    for part in range(2):
        out_ref[pl.ds(part, total, stride=2), :] = recv[
            1, :, part * lanes:(part + 1) * lanes
        ].astype(jnp.float32)
    for round_no in range(2):
        for hop in range(depth):
            for copy in swap_targets(round_no, hop):
                copy.wait_send()
    for build, guard in started:
        finish(build, guard)


def shards_in_kernel(stem_tensor, sub_branches, branch_bits):
    count = lax.axis_size("wide")
    depth = count // 2
    lanes = 2**lane_bits
    total = stem_tensor.shape[1] // lanes
    dim = sub_branches.shape[-1]
    stem = stem_tensor.reshape(2, total, lanes).transpose(1, 0, 2).reshape(2 * total, lanes)
    vmem = pl.BlockSpec(memory_space=pltpu.VMEM)
    hbm = pl.BlockSpec(memory_space=pl.ANY)
    slots = 2 * depth - 1
    semaphores = [(BRANCHES, 2)]
    for shape in ((2, BRANCHES, depth), (BRANCHES, slots + 1), (BRANCHES, 2, slots),
                  (BRANCHES, 2, 2, slots), (2, 2 * count)):
        semaphores += [shape, shape]
    result = pl.pallas_call(
        functools.partial(stem_kernel, count),
        out_shape=jax.ShapeDtypeStruct((2 * total, lanes), jnp.float32),
        in_specs=[pl.BlockSpec(memory_space=pltpu.SMEM), hbm, hbm],
        out_specs=vmem,
        scratch_shapes=[
            pltpu.VMEM((2, BRANCHES, 2, dim, dim), jnp.bfloat16),
            pltpu.VMEM((2, dim, 2 * dim), jnp.bfloat16),
            pltpu.VMEM((total, 2 * lanes), jnp.bfloat16),
            pltpu.VMEM((total, 2 * lanes), jnp.bfloat16),
            pltpu.VMEM((2, total, 2 * lanes), jnp.bfloat16),
            pltpu.VMEM((2, total, 2 * lanes), jnp.bfloat16),
            pltpu.VMEM((2 * total, lanes), jnp.float32),
            pltpu.SemaphoreType.DMA(()),
        ] + [pltpu.SemaphoreType.DMA(shape) for shape in semaphores],
        compiler_params=pltpu.CompilerParams(collective_id=0, has_side_effects=True),
    )(branch_bits, stem, sub_branches[:, 0])
    return result.reshape(total, 2, lanes).transpose(1, 0, 2).reshape(2, -1)


sublane_tile = 16


def solution(mesh):
    in_specs = (P(None, ("cuts", "wide", "narrow")), P(None, "narrow", None, "wide", None), P())
    out_specs = P(None, ("cuts", "wide", "narrow"))

    def run(stem_tensor, sub_branches, branch_bits):
        whole_tiles = sub_branches.shape[3] % sublane_tile == 0 and mesh.shape["cuts"] == 2
        body = shards_in_kernel if whole_tiles else shards
        return body(stem_tensor, sub_branches, branch_bits)

    return jax.shard_map(run, mesh=mesh, in_specs=in_specs, out_specs=out_specs, check_vma=False)
```
